32 devices in a mesh: groups: 2 (over y), seq: 16 (over z, x, core).
Axes of the slice: x: 2, y: 2, z: 4, core: 2. Of those that a mesh axis runs over, the one named last changes fastest.
Arguments:
- inputs: bfloat16 [16384, 768], P(('groups', 'seq')), parts along dimension 0, may hold values from -400 to 400
- projection: bfloat16 [768, 2304], P('seq'), may hold values from -2 to 2
- positions: int32 [16384], P(('groups', 'seq')), parts along dimension 0, may hold values from 0 to 1024, as said below
- segments: int32 [16384], P(('groups', 'seq')), parts along dimension 0, may hold values from 0 to 7, as said below
- context_grad: bfloat16 [16384, 768], P(('groups', 'seq')), parts along dimension 0, may hold values from -6 to 6
Outputs:
- context: bfloat16 [16384, 768], P(('groups', 'seq')), parts along dimension 0
- input_grad: bfloat16 [16384, 768], P(('groups', 'seq')), parts along dimension 0
- projection_grad: float32 [1536, 2304], P(('groups', 'seq')), parts along dimension 0
The draws below stay inside these ranges and needn't reach their ends.
There are 2 independent parts, one for each index of `groups`. The reference program is written for one: setup_inputs(seed, part) draws one part's arguments, and reference() takes and returns one part's arrays. A program takes and returns all parts, laid end to end along the dimension named above; an argument that names none is the same for every part. Nothing has to cross between parts.
Inputs may be any that keep to these rules, and one draw needn't show every extreme that they name: `segments`: segment ids never fall along the sequence; the first token has id 0, the last id 8 - 1, and every id in between occurs. positions are 0 at the first token of every segment; within a segment a position is the segment's time index capped at 1024, and the time index rises by 0 to 3 from one token to the next.
All inputs are finite; a program needn't handle non-finite values.
Results may differ from the reference program's by a relative error of at most 0.03.
The reference program's roundings to bfloat16 on the way (of `normed`, `values`, `probs`, `dscores` and `dqkv`) count: a program that leaves them out, or rounds other values in their place, can miss the bound.
Values may be sent and summed in bfloat16 or wider, within the bound.
A program may use at most 128 MiB of HBM per device.

```python
import math
import jax
import jax.numpy as jnp
from jax import lax

D = 768
H = 12
HD = 64
W = 1024
TOKENS = 8192
SEGS = 8


def segment_ids(key):
    cut_key = jax.random.fold_in(key, 11)
    cuts = jax.random.permutation(cut_key, TOKENS - W - 1)[:SEGS - 1].astype(jnp.int32) + W + 1
    places = jnp.arange(TOKENS, dtype=jnp.int32)
    return jnp.sum((places[:, None] >= cuts[None, :]).astype(jnp.int32), axis=1).astype(jnp.int32)


def tick_steps(key):
    loose = jax.random.randint(jax.random.fold_in(key, 12), (TOKENS,), 0, 4).astype(jnp.int32)
    firm = jax.random.randint(jax.random.fold_in(key, 13), (TOKENS,), 1, 4).astype(jnp.int32)
    places = jnp.arange(TOKENS, dtype=jnp.int32)
    return jnp.where(places <= W, firm, loose).astype(jnp.int32)


def draw_segments(key, part):
    return segment_ids(key)


def draw_positions(key, part):
    seg_ids = segment_ids(key)
    steps = tick_steps(key)
    before = (jnp.cumsum(steps) - steps).astype(jnp.int32)
    is_start = jnp.concatenate([jnp.ones((1,), jnp.bool_), seg_ids[1:] != seg_ids[:-1]])
    start_value = lax.cummax(jnp.where(is_start, before, 0), axis=0)
    return jnp.minimum(before - start_value, W).astype(jnp.int32)


def draw_inputs(key, part):
    base_key = jax.random.fold_in(key, 21)
    row_scale = jnp.exp(jax.random.uniform(jax.random.fold_in(key, 22), (TOKENS, 1), jnp.float32, 0.0, math.log(10.0)))
    col_scale = jnp.exp(jax.random.uniform(jax.random.fold_in(key, 23), (1, D), jnp.float32, 0.0, math.log(10.0)))
    base = jax.random.truncated_normal(base_key, -4.0, 4.0, (TOKENS, D), jnp.float32)
    return (base * row_scale * col_scale).astype(jnp.bfloat16)


def draw_projection(key, part):
    return (jax.random.truncated_normal(jax.random.fold_in(key, 33), -4.0, 4.0, (D, 3 * D), jnp.float32) / math.sqrt(D)).astype(jnp.bfloat16)


def block_levels(key, extent, shards, low, high):
    gain, own = 1.0, jax.random.fold_in(key, 6)
    for axis_at, blocks in shards:
        steps = jnp.exp(jax.random.uniform(jax.random.fold_in(own, axis_at), (blocks,), jnp.float32, low / len(shards), high / len(shards)))
        gain = gain * jnp.repeat(steps, extent[axis_at] // blocks).reshape([-1 if axis == axis_at else 1 for axis in range(len(extent))])
    return gain


def noise(stream_key, extent, width, bound, split=(), kind=jnp.bfloat16):
    entries = width * jax.random.normal(stream_key, extent, jnp.float32)
    if split:
        entries = entries * block_levels(stream_key, extent, split, -0.22, 0.18)
    return jnp.clip(entries, -bound, bound).astype(kind)


def setup_inputs(seed: int = 0, part: int = 0) -> dict:
    key_list = jax.random.split(jax.random.key(seed), 6)
    own_keys = jax.random.split(jax.random.fold_in(key_list[5], part), 6)
    return {
        "inputs": draw_inputs(jax.random.fold_in(jax.random.fold_in(key_list[5], part), 71), part),
        "projection": draw_projection(jax.random.fold_in(key_list[5], 71), part),
        "positions": draw_positions(jax.random.fold_in(jax.random.fold_in(key_list[5], part), 71), part),
        "segments": draw_segments(jax.random.fold_in(jax.random.fold_in(key_list[5], part), 71), part),
        "context_grad": noise(own_keys[4], (TOKENS, D), 1.0, 6.0, ((0, 16),)),
    }


EPSILON = 1e-05
SCORE_SCALE = 0.125
MASKED_SCORE = -1e+30

def rotary_tables(positions):
    half_size = HD // 2
    frequency = jnp.exp(-math.log(10000.0) * jnp.arange(half_size, dtype=jnp.float32) / half_size)
    angle = positions.astype(jnp.float32)[:, None] * frequency[None, :]
    return (jnp.cos(angle)[:, None, :], jnp.sin(angle)[:, None, :])

def rotate(tensor, cosine_table, sine_table):
    first_half = tensor[..., :HD // 2]
    second_half = tensor[..., HD // 2:]
    return jnp.concatenate([first_half * cosine_table - second_half * sine_table, second_half * cosine_table + first_half * sine_table], axis=-1)

def unrotate(tensor, cosine_table, sine_table):
    first_half = tensor[..., :HD // 2]
    second_half = tensor[..., HD // 2:]
    return jnp.concatenate([first_half * cosine_table + second_half * sine_table, second_half * cosine_table - first_half * sine_table], axis=-1)

def reference(inputs, projection, positions, segments, context_grad):
    x_float = inputs.astype(jnp.float32)
    inv_rms = lax.rsqrt(lax.optimization_barrier(jnp.mean(x_float * x_float, axis=1, keepdims=True)) + EPSILON)
    scaled = x_float * inv_rms
    normed = scaled.astype(jnp.bfloat16)
    projected = jnp.dot(normed, projection, preferred_element_type=jnp.float32)
    cosine_table, sine_table = rotary_tables(positions)
    q_rot = rotate(projected[:, :D].reshape(TOKENS, H, HD), cosine_table, sine_table).astype(jnp.bfloat16)
    k_rot = rotate(projected[:, D:2 * D].reshape(TOKENS, H, HD), cosine_table, sine_table).astype(jnp.bfloat16)
    values = projected[:, 2 * D:].reshape(TOKENS, H, HD).astype(jnp.bfloat16)
    out_grads = context_grad.reshape(TOKENS, H, HD)
    key_padded = jnp.concatenate([jnp.zeros((W, H, HD), jnp.bfloat16), k_rot], axis=0)
    value_padded = jnp.concatenate([jnp.zeros((W, H, HD), jnp.bfloat16), values], axis=0)
    seg_padded = jnp.concatenate([jnp.full((W,), -1, jnp.int32), segments.astype(jnp.int32)], axis=0)
    block_rows = min(256, TOKENS)
    block_count = TOKENS // block_rows
    key_span = block_rows + W
    offsets = jnp.arange(block_rows, dtype=jnp.int32)[:, None] + W - jnp.arange(key_span, dtype=jnp.int32)[None, :]

    def visit(carry, number):
        key_acc, value_acc = carry
        first_row = number * block_rows
        queries = lax.dynamic_slice_in_dim(q_rot, first_row, block_rows, 0)
        grad_rows = lax.dynamic_slice_in_dim(out_grads, first_row, block_rows, 0)
        query_seg = lax.dynamic_slice_in_dim(segments.astype(jnp.int32), first_row, block_rows, 0)
        key_block = lax.dynamic_slice_in_dim(key_padded, first_row, key_span, 0)
        value_block = lax.dynamic_slice_in_dim(value_padded, first_row, key_span, 0)
        key_seg = lax.dynamic_slice_in_dim(seg_padded, first_row, key_span, 0)
        allowed = (offsets >= 0) & (offsets < W) & (query_seg[:, None] == key_seg[None, :])
        scores = jnp.einsum('qhe,khe->hqk', queries.astype(jnp.float32), key_block.astype(jnp.float32)) * SCORE_SCALE
        masked = jnp.where(allowed[None], scores, MASKED_SCORE)
        row_max = lax.optimization_barrier(jnp.max(masked, axis=2, keepdims=True))
        log_total = row_max + jnp.log(lax.optimization_barrier(jnp.sum(jnp.exp(masked - row_max), axis=2, keepdims=True)))
        weights = jnp.exp(masked - log_total)
        probs = weights.astype(jnp.bfloat16)
        context = jnp.einsum('hqk,khe->qhe', probs.astype(jnp.float32), value_block.astype(jnp.float32)).astype(jnp.bfloat16)
        row_delta = lax.optimization_barrier(jnp.sum(grad_rows.astype(jnp.float32) * context.astype(jnp.float32), axis=2))
        dprobs = jnp.einsum('qhe,khe->hqk', grad_rows.astype(jnp.float32), value_block.astype(jnp.float32))
        dscores = (weights * (dprobs - jnp.transpose(row_delta)[:, :, None])).astype(jnp.bfloat16)
        query_grad = jnp.einsum('hqk,khe->qhe', dscores.astype(jnp.float32), key_block.astype(jnp.float32)) * SCORE_SCALE
        key_grad = jnp.einsum('hqk,qhe->khe', dscores.astype(jnp.float32), queries.astype(jnp.float32)) * SCORE_SCALE
        value_grad = jnp.einsum('hqk,qhe->khe', probs.astype(jnp.float32), grad_rows.astype(jnp.float32))
        key_acc = lax.dynamic_update_slice_in_dim(key_acc, lax.dynamic_slice_in_dim(key_acc, first_row, key_span, 0) + key_grad, first_row, 0)
        value_acc = lax.dynamic_update_slice_in_dim(value_acc, lax.dynamic_slice_in_dim(value_acc, first_row, key_span, 0) + value_grad, first_row, 0)
        return ((key_acc, value_acc), (context, query_grad))
    start_acc = (jnp.zeros((TOKENS + W, H, HD), jnp.float32), jnp.zeros((TOKENS + W, H, HD), jnp.float32))
    (key_acc, value_acc), (context_blocks, query_blocks) = lax.scan(visit, start_acc, jnp.arange(block_count, dtype=jnp.int32))
    context = context_blocks.reshape(TOKENS, D)
    query_grad = query_blocks.reshape(TOKENS, H, HD)
    query_lin = unrotate(query_grad, cosine_table, sine_table).reshape(TOKENS, D)
    key_lin = unrotate(key_acc[W:], cosine_table, sine_table).reshape(TOKENS, D)
    value_lin = value_acc[W:].reshape(TOKENS, D)
    dqkv = jnp.concatenate([query_lin, key_lin, value_lin], axis=1).astype(jnp.bfloat16)
    normed_grad = jnp.dot(dqkv, projection.T, preferred_element_type=jnp.float32)
    input_grad = (inv_rms * (normed_grad - scaled * lax.optimization_barrier(jnp.mean(normed_grad * scaled, axis=1, keepdims=True)))).astype(jnp.bfloat16)
    projection_grad = jnp.dot(normed.T, dqkv, preferred_element_type=jnp.float32) * TOKENS ** (-0.5)
    return (context, input_grad, projection_grad)
```

```python
import functools
import math

import jax
import jax.numpy as jnp
from jax import lax
from jax.experimental import pallas as pl
from jax.experimental.pallas import tpu as pltpu
from jax.sharding import PartitionSpec as P

D = 768
H = 12
HD = 64
W = 1024
EPSILON = 1e-05
SCORE_SCALE = 0.125
MASKED_SCORE = -1e30
BLOCK = 256
SPAN = BLOCK + W
PAIR = 2 * HD
HALF = D // 2


def contract(a, b, da, db):
    return lax.dot_general(a, b, (((da,), (db,)), ((), ())), preferred_element_type=jnp.float32)


def attention_kernel(
    core_ref, nx_ref, wq_ref, wk_ref, wv_ref, cos_ref, sin_ref, segq_ref, segk_ref, do_ref,
    ctx_ref, dq_ref, dk_ref, dv_ref,
    bias, qs, ks, vs, dka, dva,
):
    own = ctx_ref.shape[0]
    total = nx_ref.shape[0]
    lane = lax.broadcasted_iota(jnp.int32, (1, PAIR), 1)
    low = (lane % HD) < HD // 2

    def swap(u):
        return jnp.where(low, pltpu.roll(u, PAIR - HD // 2, 1), pltpu.roll(u, HD // 2, 1))

    @pl.when(pl.program_id(0) == 0)
    def _():
        row = lax.broadcasted_iota(jnp.int32, (BLOCK, SPAN), 0)
        col = lax.broadcasted_iota(jnp.int32, (BLOCK, SPAN), 1)
        near = (col > row) & (col <= row + W)
        for b in range(own // BLOCK):
            same = segq_ref[b * BLOCK : (b + 1) * BLOCK, :] == segk_ref[:, b * BLOCK : b * BLOCK + SPAN]
            bias[b] = jnp.where(near & same, 0.0, MASKED_SCORE)

    def project(i, carry):
        rows = pl.ds(pl.multiple_of(i * BLOCK, BLOCK), BLOCK)
        x = nx_ref[rows, :]
        k = contract(x, wk_ref[...], 1, 0)
        ks[rows, :] = (k * cos_ref[rows, :] + swap(k) * sin_ref[rows, :]).astype(jnp.bfloat16)
        vs[rows, :] = contract(x, wv_ref[...], 1, 0).astype(jnp.bfloat16)
        dka[rows, :] = jnp.zeros((BLOCK, PAIR), jnp.float32)
        dva[rows, :] = jnp.zeros((BLOCK, PAIR), jnp.float32)
        return carry

    lax.fori_loop(0, total // BLOCK, project, 0)

    def query(i, carry):
        rows = pl.ds(pl.multiple_of(i * BLOCK, BLOCK), BLOCK)
        here = pl.ds(pl.multiple_of(i * BLOCK + W, BLOCK), BLOCK)
        q = contract(nx_ref[here, :], wq_ref[...], 1, 0)
        q = (q * cos_ref[here, :] + swap(q) * sin_ref[here, :]).astype(jnp.bfloat16)
        qs[rows, :] = q * jnp.bfloat16(SCORE_SCALE)
        return carry

    lax.fori_loop(0, own // BLOCK, query, 0)

    def visit(b, carry):
        rows = pl.ds(pl.multiple_of(b * BLOCK, BLOCK), BLOCK)
        here = pl.ds(pl.multiple_of(b * BLOCK + W, BLOCK), BLOCK)
        window = pl.ds(pl.multiple_of(b * BLOCK, BLOCK), SPAN)
        contexts, grads = [], []
        for h in range(2):
            mine = (lane // HD) == h
            kb = ks[window, :]
            vb = vs[window, :]
            qh = jnp.where(mine, qs[rows, :], jnp.bfloat16(0))
            gh = jnp.where(mine, do_ref[rows, :], jnp.bfloat16(0))
            s = contract(qh, kb, 1, 1) + bias[b]
            e = jnp.exp(s - jnp.max(s, axis=1, keepdims=True))
            w = e * (1.0 / jnp.sum(e, axis=1, keepdims=True))
            pb = w.astype(jnp.bfloat16)
            context = contract(pb, vb, 1, 0).astype(jnp.bfloat16)
            delta = jnp.sum(
                gh.astype(jnp.float32) * context.astype(jnp.float32), axis=1, keepdims=True
            )
            dp = contract(gh, vb, 1, 1)
            ds = (w * (dp - delta)).astype(jnp.bfloat16)
            contexts.append(context)
            grads.append(contract(ds, kb, 1, 0))
            dka[window, :] += contract(ds, qh, 0, 0)
            dva[window, :] += contract(pb, gh, 0, 0)
        first = lane < HD
        ctx_ref[rows, :] = jnp.where(first, contexts[0], contexts[1])
        g = jnp.where(first, grads[0], grads[1]) * SCORE_SCALE
        dq_ref[rows, :] = (g * cos_ref[here, :] - swap(g) * sin_ref[here, :]).astype(jnp.bfloat16)
        return carry

    lax.fori_loop(0, own // BLOCK, visit, 0)

    def finish(i, carry):
        rows = pl.ds(pl.multiple_of(i * BLOCK, BLOCK), BLOCK)
        g = dka[rows, :]
        dk_ref[rows, :] = (g * cos_ref[rows, :] - swap(g) * sin_ref[rows, :]).astype(jnp.bfloat16)
        dv_ref[rows, :] = dva[rows, :].astype(jnp.bfloat16)
        return carry

    lax.fori_loop(0, total // BLOCK, finish, 0)


def attention(core, nx, weights, cosine, sine, seg_q, seg_k, out_grads):
    total = nx.shape[0]
    own = total - W
    pairs = HALF // PAIR

    def whole(shape):
        return pl.BlockSpec(shape, lambda p, c: (0, 0))

    def columns(start):
        return pl.BlockSpec((D, PAIR), lambda p, c: (0, start + c[0] * pairs + p))

    def heads(rows):
        return pl.BlockSpec((rows, PAIR), lambda p, c: (0, p))

    return pl.pallas_call(
        attention_kernel,
        out_shape=[
            jax.ShapeDtypeStruct((own, HALF), jnp.bfloat16),
            jax.ShapeDtypeStruct((own, HALF), jnp.bfloat16),
            jax.ShapeDtypeStruct((total, HALF), jnp.bfloat16),
            jax.ShapeDtypeStruct((total, HALF), jnp.bfloat16),
        ],
        grid_spec=pltpu.PrefetchScalarGridSpec(
            num_scalar_prefetch=1,
            grid=(pairs,),
            in_specs=[
                whole((total, D)),
                columns(0),
                columns(2 * pairs),
                columns(4 * pairs),
                whole((total, PAIR)),
                whole((total, PAIR)),
                whole((own, 1)),
                whole((1, total)),
                heads(own),
            ],
            out_specs=[heads(own), heads(own), heads(total), heads(total)],
            scratch_shapes=[
                pltpu.VMEM((own // BLOCK, BLOCK, SPAN), jnp.float32),
                pltpu.VMEM((own, PAIR), jnp.bfloat16),
                pltpu.VMEM((total, PAIR), jnp.bfloat16),
                pltpu.VMEM((total, PAIR), jnp.bfloat16),
                pltpu.VMEM((total, PAIR), jnp.float32),
                pltpu.VMEM((total, PAIR), jnp.float32),
            ],
        ),
        compiler_params=pltpu.CompilerParams(vmem_limit_bytes=48 * 1024 * 1024),
        name="window_attention",
    )(core, nx, weights, weights, weights, cosine, sine, seg_q, seg_k, out_grads)


def swapped(value):
    count = lax.axis_size("seq")
    return lax.ppermute(value, "seq", [(s, s ^ 1) for s in range(count)])


def chip_shifted(value, steps):
    count = lax.axis_size("seq")
    pairs = [(s, s + 2 * steps) for s in range(count) if 0 <= s + 2 * steps < count]
    return lax.ppermute(value, "seq", pairs)


def ordered(core, mine, other, axis=0):
    first = jnp.where(core == 0, mine, other)
    second = jnp.where(core == 0, other, mine)
    return jnp.concatenate([first, second], axis=axis)


def local(inputs, projection, positions, segments, context_grad):
    row_count = inputs.shape[0]
    device_count = lax.axis_size("seq")
    chips = device_count // 2
    device_index = lax.axis_index("seq")
    core = device_index % 2
    chip = device_index // 2
    assert 2 * row_count == W
    grad_scale = (row_count * device_count) ** (-0.5)

    weights = lax.all_gather(projection, "seq", axis=0, tiled=True)

    meta = jnp.stack([positions, segments], axis=0)
    x_before = chip_shifted(inputs, 1)
    meta_before = chip_shifted(meta, 1)
    x_other = swapped(inputs)
    meta_other = swapped(meta)
    x_before_other = swapped(x_before)
    meta_before_other = swapped(meta_before)
    grad_mine = lax.dynamic_slice_in_dim(context_grad, core * HALF, HALF, 1)
    grad_sent = lax.dynamic_slice_in_dim(context_grad, (1 - core) * HALF, HALF, 1)
    grad_other = swapped(grad_sent)
    out_grads = ordered(core, grad_mine, grad_other)

    x_all = jnp.concatenate(
        [ordered(core, x_before, x_before_other), ordered(core, inputs, x_other)], axis=0
    ).astype(jnp.float32)
    nx = (
        x_all * lax.rsqrt(jnp.mean(x_all * x_all, axis=1, keepdims=True) + EPSILON)
    ).astype(jnp.bfloat16)
    meta_all = jnp.concatenate(
        [ordered(core, meta_before, meta_before_other, 1), ordered(core, meta, meta_other, 1)],
        axis=1,
    )
    half_size = HD // 2
    frequency = jnp.exp(-math.log(10000.0) * jnp.arange(half_size, dtype=jnp.float32) / half_size)
    angle = meta_all[0].astype(jnp.float32)[:, None] * frequency[None, :]
    c, s = jnp.cos(angle), jnp.sin(angle)
    cosine = jnp.concatenate([c, c, c, c], axis=1)
    sine = jnp.concatenate([-s, s, -s, s], axis=1)
    seg_all = meta_all[1]
    outside = (jnp.arange(seg_all.shape[0]) < W) & (chip == 0)
    seg_k = jnp.where(outside, -1, seg_all)[None, :]
    seg_q = seg_all[W:][:, None]

    context_heads, dq, dk, dv = attention(
        core.astype(jnp.int32)[None], nx, weights, cosine, sine, seg_q, seg_k, out_grads
    )

    mine_at = core * row_count
    other_at = (1 - core) * row_count
    context_mine = lax.dynamic_slice_in_dim(context_heads, mine_at, row_count, 0)
    context_other = swapped(lax.dynamic_slice_in_dim(context_heads, other_at, row_count, 0))
    context = ordered(core, context_mine, context_other, 1)

    w_q, w_k, w_v = [
        lax.dynamic_slice_in_dim(weights, t * D + core * HALF, HALF, 1) for t in range(3)
    ]
    dkv = jnp.concatenate([dk, dv], axis=1)
    w_kv = jnp.concatenate([w_k, w_v], axis=1)
    ng_kv = contract(dkv, w_kv, 1, 1)
    ng_q = contract(dq, w_q, 1, 1)
    ng_before = ng_kv[:W]
    ng_own = ng_kv[W:] + ng_q
    send_before = lax.dynamic_slice_in_dim(ng_before, other_at, row_count, 0).astype(jnp.bfloat16)
    keep_before = lax.dynamic_slice_in_dim(ng_before, mine_at, row_count, 0)
    before = keep_before + swapped(send_before).astype(jnp.float32)
    later = chip_shifted(before.astype(jnp.bfloat16), -1)
    send_own = lax.dynamic_slice_in_dim(ng_own, other_at, row_count, 0).astype(jnp.bfloat16)
    keep_own = lax.dynamic_slice_in_dim(ng_own, mine_at, row_count, 0)
    normed_grad = (
        keep_own + swapped(send_own).astype(jnp.float32) + later.astype(jnp.float32)
    )
    x_float = inputs.astype(jnp.float32)
    inv_rms = lax.rsqrt(jnp.mean(x_float * x_float, axis=1, keepdims=True) + EPSILON)
    scaled = x_float * inv_rms
    input_grad = (
        inv_rms * (normed_grad - scaled * jnp.mean(normed_grad * scaled, axis=1, keepdims=True))
    ).astype(jnp.bfloat16)

    pg_kv = contract(nx, dkv, 0, 0)
    pg_q = contract(nx[W:], dq, 0, 0)
    pg = jnp.concatenate([pg_q, pg_kv], axis=1).astype(jnp.bfloat16)
    groups = [[2 * i + k for i in range(chips)] for k in range(2)]
    summed = lax.psum_scatter(
        pg, "seq", scatter_dimension=0, axis_index_groups=groups, tiled=True
    ).astype(jnp.float32)
    rows = summed.shape[0] // 2
    keep = lax.dynamic_slice_in_dim(summed, core * rows, rows, 0)
    other = swapped(lax.dynamic_slice_in_dim(summed, (1 - core) * rows, rows, 0).astype(jnp.bfloat16))
    other = other.astype(jnp.float32)
    parts = []
    for t in range(3):
        cols = slice(t * HALF, (t + 1) * HALF)
        parts.append(ordered(core, keep[:, cols], other[:, cols], 1))
    projection_grad = jnp.concatenate(parts, axis=1) * grad_scale
    return (context, input_grad, projection_grad)


def solution(mesh):
    in_specs = (
        P(("groups", "seq"), None),
        P("seq", None),
        P(("groups", "seq")),
        P(("groups", "seq")),
        P(("groups", "seq"), None),
    )
    out_specs = (P(("groups", "seq"), None), P(("groups", "seq"), None), P(("groups", "seq"), None))
    return jax.shard_map(local, mesh=mesh, in_specs=in_specs, out_specs=out_specs, check_vma=False)
```

```python
import functools
import math

import jax
import jax.numpy as jnp
from jax import lax
from jax.experimental import pallas as pl
from jax.experimental.pallas import tpu as pltpu
from jax.sharding import PartitionSpec as P

D = 768
H = 12
HD = 64
W = 1024
EPSILON = 1e-05
SCORE_SCALE = 0.125
MASKED_SCORE = -1e30
BLOCK = 256
SPAN = BLOCK + W
PAIR = 2 * HD
HALF = D // 2


def contract(a, b, da, db):
    return lax.dot_general(a, b, (((da,), (db,)), ((), ())), preferred_element_type=jnp.float32)


def swap_halves(u, lane):
    low = (lane % HD) < HD // 2
    return jnp.where(low, pltpu.roll(u, PAIR - HD // 2, 1), pltpu.roll(u, HD // 2, 1))


def pair_attention(
    p, nx_ref, wq_ref, wk_ref, wv_ref, cos_ref, sin_ref, segq_ref, segk_ref, do_ref,
    ctx_ref, dq_ref,
    bias, qs, ks, vs, dka, dva,
):
    own = ctx_ref.shape[0]
    total = nx_ref.shape[0]
    lane = lax.broadcasted_iota(jnp.int32, (1, PAIR), 1)

    def swap(u):
        return swap_halves(u, lane)

    @pl.when(p == 0)
    def _():
        row = lax.broadcasted_iota(jnp.int32, (BLOCK, SPAN), 0)
        col = lax.broadcasted_iota(jnp.int32, (BLOCK, SPAN), 1)
        near = (col > row) & (col <= row + W)
        for b in range(own // BLOCK):
            same = segq_ref[b * BLOCK : (b + 1) * BLOCK, :] == segk_ref[:, b * BLOCK : b * BLOCK + SPAN]
            bias[b] = jnp.where(near & same, 0.0, MASKED_SCORE)

    def project(i, carry):
        rows = pl.ds(pl.multiple_of(i * BLOCK, BLOCK), BLOCK)
        x = nx_ref[rows, :]
        k = contract(x, wk_ref[...], 1, 0)
        ks[rows, :] = (k * cos_ref[rows, :] + swap(k) * sin_ref[rows, :]).astype(jnp.bfloat16)
        vs[rows, :] = contract(x, wv_ref[...], 1, 0).astype(jnp.bfloat16)
        dka[rows, :] = jnp.zeros((BLOCK, PAIR), jnp.float32)
        dva[rows, :] = jnp.zeros((BLOCK, PAIR), jnp.float32)
        return carry

    lax.fori_loop(0, total // BLOCK, project, 0)

    def query(i, carry):
        rows = pl.ds(pl.multiple_of(i * BLOCK, BLOCK), BLOCK)
        here = pl.ds(pl.multiple_of(i * BLOCK + W, BLOCK), BLOCK)
        q = contract(nx_ref[here, :], wq_ref[...], 1, 0)
        q = (q * cos_ref[here, :] + swap(q) * sin_ref[here, :]).astype(jnp.bfloat16)
        qs[rows, :] = q * jnp.bfloat16(SCORE_SCALE)
        return carry

    lax.fori_loop(0, own // BLOCK, query, 0)

    def visit(b, carry):
        rows = pl.ds(pl.multiple_of(b * BLOCK, BLOCK), BLOCK)
        here = pl.ds(pl.multiple_of(b * BLOCK + W, BLOCK), BLOCK)
        window = pl.ds(pl.multiple_of(b * BLOCK, BLOCK), SPAN)
        contexts, grads = [], []
        for h in range(2):
            mine = (lane // HD) == h
            kb = ks[window, :]
            vb = vs[window, :]
            qh = jnp.where(mine, qs[rows, :], jnp.bfloat16(0))
            gh = jnp.where(mine, do_ref[rows, :], jnp.bfloat16(0))
            s = contract(qh, kb, 1, 1) + bias[b]
            e = jnp.exp(s - jnp.max(s, axis=1, keepdims=True))
            w = e * (1.0 / jnp.sum(e, axis=1, keepdims=True))
            pb = w.astype(jnp.bfloat16)
            context = contract(pb, vb, 1, 0).astype(jnp.bfloat16)
            delta = jnp.sum(
                gh.astype(jnp.float32) * context.astype(jnp.float32), axis=1, keepdims=True
            )
            dp = contract(gh, vb, 1, 1)
            ds = (w * (dp - delta)).astype(jnp.bfloat16)
            contexts.append(context)
            grads.append(contract(ds, kb, 1, 0))
            dka[window, :] += contract(ds, qh, 0, 0)
            dva[window, :] += contract(pb, gh, 0, 0)
        first = lane < HD
        ctx_ref[rows, :] = jnp.where(first, contexts[0], contexts[1])
        g = jnp.where(first, grads[0], grads[1]) * SCORE_SCALE
        dq_ref[rows, :] = (g * cos_ref[here, :] - swap(g) * sin_ref[here, :]).astype(jnp.bfloat16)
        return carry

    lax.fori_loop(0, own // BLOCK, visit, 0)


def attention_kernel(
    core_ref, nx_ref, wq_ref, wk_ref, wv_ref, cos_ref, sin_ref, segq_ref, segk_ref, do_ref,
    ctx_ref, dq_ref, dk_ref, dv_ref,
    bias, qs, ks, vs, dka, dva,
):
    total = nx_ref.shape[0]
    lane = lax.broadcasted_iota(jnp.int32, (1, PAIR), 1)

    def swap(u):
        return swap_halves(u, lane)

    pair_attention(
        pl.program_id(0), nx_ref, wq_ref, wk_ref, wv_ref, cos_ref, sin_ref, segq_ref, segk_ref,
        do_ref, ctx_ref, dq_ref, bias, qs, ks, vs, dka, dva,
    )

    def finish(i, carry):
        rows = pl.ds(pl.multiple_of(i * BLOCK, BLOCK), BLOCK)
        g = dka[rows, :]
        dk_ref[rows, :] = (g * cos_ref[rows, :] - swap(g) * sin_ref[rows, :]).astype(jnp.bfloat16)
        dv_ref[rows, :] = dva[rows, :].astype(jnp.bfloat16)
        return carry

    lax.fori_loop(0, total // BLOCK, finish, 0)


def attention(core, nx, weights, cosine, sine, seg_q, seg_k, out_grads):
    total = nx.shape[0]
    own = total - W
    pairs = HALF // PAIR

    def whole(shape):
        return pl.BlockSpec(shape, lambda p, c: (0, 0))

    def columns(start):
        return pl.BlockSpec((D, PAIR), lambda p, c: (0, start + c[0] * pairs + p))

    def heads(rows):
        return pl.BlockSpec((rows, PAIR), lambda p, c: (0, p))

    return pl.pallas_call(
        attention_kernel,
        out_shape=[
            jax.ShapeDtypeStruct((own, HALF), jnp.bfloat16),
            jax.ShapeDtypeStruct((own, HALF), jnp.bfloat16),
            jax.ShapeDtypeStruct((total, HALF), jnp.bfloat16),
            jax.ShapeDtypeStruct((total, HALF), jnp.bfloat16),
        ],
        grid_spec=pltpu.PrefetchScalarGridSpec(
            num_scalar_prefetch=1,
            grid=(pairs,),
            in_specs=[
                whole((total, D)),
                columns(0),
                columns(2 * pairs),
                columns(4 * pairs),
                whole((total, PAIR)),
                whole((total, PAIR)),
                whole((own, 1)),
                whole((1, total)),
                heads(own),
            ],
            out_specs=[heads(own), heads(own), heads(total), heads(total)],
            scratch_shapes=[
                pltpu.VMEM((own // BLOCK, BLOCK, SPAN), jnp.float32),
                pltpu.VMEM((own, PAIR), jnp.bfloat16),
                pltpu.VMEM((total, PAIR), jnp.bfloat16),
                pltpu.VMEM((total, PAIR), jnp.bfloat16),
                pltpu.VMEM((total, PAIR), jnp.float32),
                pltpu.VMEM((total, PAIR), jnp.float32),
            ],
        ),
        compiler_params=pltpu.CompilerParams(vmem_limit_bytes=48 * 1024 * 1024),
        name="window_attention",
    )(core, nx, weights, weights, weights, cosine, sine, seg_q, seg_k, out_grads)


def fused_kernel(
    nx_ref, wq_ref, wk_ref, wv_ref, cos_ref, sin_ref, segq_ref, segk_ref, do_ref,
    ctx_ref, ng_ref, pg_ref,
    bias, qs, ks, vs, dka, dva, dqs, dkv, ctxs, ctxr, acc, part, sums, xs, xr, ys, yr, fwd, later,
    part_send, part_recv, ctx_send, ctx_recv, x_send, x_recv, fwd_send, fwd_recv,
    *, count, grad_scale,
):
    p = pl.program_id(0)
    last = pl.num_programs(0) - 1
    me = lax.axis_index("seq")
    core = lax.rem(me, 2)
    partner = me + 1 - 2 * core
    total = nx_ref.shape[0]
    own = total - W
    half = own // 2
    share = D // count
    chunks = xs.shape[0]
    piece = half // chunks
    mine_at = pl.multiple_of(core * half, half)
    other_at = pl.multiple_of((1 - core) * half, half)

    def remote(source, target, send, recv, device):
        return pltpu.make_async_remote_copy(
            src_ref=source, dst_ref=target, send_sem=send, recv_sem=recv,
            device_id={"seq": device}, device_id_type=pl.DeviceIdType.MESH,
        )

    @pl.when(p == 0)
    def _():
        barrier = pltpu.get_barrier_semaphore()

        def greet(i, carry):
            pl.semaphore_signal(
                barrier, inc=1, device_id={"seq": lax.rem(me + 1 + i, count)},
                device_id_type=pl.DeviceIdType.MESH,
            )
            return carry

        lax.fori_loop(0, count - 1, greet, 0)
        pl.semaphore_wait(barrier, count - 1)

    pair_attention(
        p, nx_ref, wq_ref, wk_ref, wv_ref, cos_ref, sin_ref, segq_ref, segk_ref, do_ref,
        ctxs.at[p], dqs, bias, qs, ks, vs, dka, dva,
    )

    def ctx_copy(pair):
        return remote(
            ctxs.at[pair, pl.ds(other_at, half), :], ctxr.at[pair],
            ctx_send.at[pair], ctx_recv.at[pair], partner,
        )

    ctx_copy(p).start()

    lane = lax.broadcasted_iota(jnp.int32, (1, PAIR), 1)
    wkv = jnp.concatenate([wk_ref[...], wv_ref[...]], axis=1)

    def finish(i, carry):
        rows = pl.ds(pl.multiple_of(i * BLOCK, BLOCK), BLOCK)
        g = dka[rows, :]
        dk = (g * cos_ref[rows, :] - swap_halves(g, lane) * sin_ref[rows, :]).astype(jnp.bfloat16)
        block = jnp.concatenate([dk, dva[rows, :].astype(jnp.bfloat16)], axis=1)
        dkv[rows, :] = block
        grown = contract(block, wkv, 1, 1)

        @pl.when(p == 0)
        def _():
            acc[rows, :] = grown

        @pl.when(p > 0)
        def _():
            acc[rows, :] += grown

        return carry

    lax.fori_loop(0, total // BLOCK, finish, 0)

    def finish_query(i, carry):
        rows = pl.ds(pl.multiple_of(i * BLOCK, BLOCK), BLOCK)
        here = pl.ds(pl.multiple_of(i * BLOCK + W, BLOCK), BLOCK)
        acc[here, :] += contract(dqs[rows, :], wq_ref[...], 1, 1)
        return carry

    lax.fori_loop(0, own // BLOCK, finish_query, 0)

    def x_copy(j):
        return remote(xs.at[j], xr.at[j], x_send.at[j], x_recv.at[j], partner)

    def own_copy():
        return remote(
            ys, yr, x_send.at[chunks], x_recv.at[chunks], partner
        )

    @pl.when(p == last)
    def _():
        for j in range(chunks):
            xs[j] = acc[pl.ds(other_at + j * piece, piece), :].astype(jnp.bfloat16)
            x_copy(j).start()
        ys[...] = acc[pl.ds(W + other_at, half), :].astype(jnp.bfloat16)
        own_copy().start()

    def project_grad(j, carry):
        cols = pl.ds(pl.multiple_of(j * BLOCK, BLOCK), BLOCK)
        part[p, cols, :PAIR] = contract(nx_ref[W:, cols], dqs[...], 0, 0).astype(jnp.bfloat16)
        part[p, cols, PAIR:] = contract(nx_ref[:, cols], dkv[...], 0, 0).astype(jnp.bfloat16)
        return carry

    lax.fori_loop(0, D // BLOCK, project_grad, 0)

    def fwd_copy(j):
        return remote(fwd.at[j], later.at[j], fwd_send.at[j], fwd_recv.at[j], lax.rem(me + count - 2, count))

    @pl.when(p == last)
    def _():
        for j in range(chunks):
            x_copy(j).wait_recv()
            mine = acc[pl.ds(mine_at + j * piece, piece), :]
            fwd[j] = (mine + xr[j].astype(jnp.float32)).astype(jnp.bfloat16)

            @pl.when(me >= 2)
            def _():
                fwd_copy(j).start()

    def part_copy(pair, i):
        target = lax.rem(me + 1 + i, count)
        return remote(
            part.at[pair, pl.ds(pl.multiple_of(target * share, share), share), :],
            sums.at[pair, i], part_send.at[pair, i], part_recv.at[pair, i], target,
        )

    def send_part(i, carry):
        part_copy(p, i).start()
        return carry

    lax.fori_loop(0, count - 1, send_part, 0)

    @pl.when(p == last)
    def _():
        for pair in range(3):
            ctx_copy(pair).wait()
            mine_cols = pl.ds(pl.multiple_of(core * HALF + pair * PAIR, PAIR), PAIR)
            other_cols = pl.ds(pl.multiple_of((1 - core) * HALF + pair * PAIR, PAIR), PAIR)
            ctx_ref[:, mine_cols] = ctxs[pair, pl.ds(mine_at, half), :]
            ctx_ref[:, other_cols] = ctxr[pair]

        def sum_pair(pair):
            def arrive(i, carry):
                part_copy(pair, i).wait()
                return carry

            lax.fori_loop(0, count - 1, arrive, 0)

            def add(i, carry):
                odd, even = carry
                return (
                    odd + sums[pair, 2 * i].astype(jnp.float32),
                    even + sums[pair, 2 * i + 1].astype(jnp.float32),
                )

            kept = part[pair, pl.ds(pl.multiple_of(me * share, share), share), :]
            odd, even = lax.fori_loop(
                0, count // 2 - 1, add,
                (jnp.zeros((share, 3 * PAIR), jnp.float32), kept.astype(jnp.float32)),
            )
            odd = odd + sums[pair, count - 2].astype(jnp.float32)
            for t in range(3):
                at = t * D + pair * PAIR
                a = pl.ds(pl.multiple_of(at + core * HALF, PAIR), PAIR)
                b = pl.ds(pl.multiple_of(at + (1 - core) * HALF, PAIR), PAIR)
                pg_ref[:, a] = even[:, t * PAIR : (t + 1) * PAIR] * grad_scale
                pg_ref[:, b] = odd[:, t * PAIR : (t + 1) * PAIR] * grad_scale

        sum_pair(0)
        sum_pair(1)
        own_copy().wait()
        for j in range(chunks):
            x_copy(j).wait_send()
        ng_ref[...] = acc[pl.ds(W + mine_at, half), :] + yr[...].astype(jnp.float32)
        sum_pair(2)
        for j in range(chunks):

            @pl.when(me >= 2)
            def _():
                fwd_copy(j).wait_send()

            @pl.when(me < count - 2)
            def _():
                fwd_copy(j).wait_recv()
                ng_ref[j * piece : (j + 1) * piece, :] += later[j].astype(jnp.float32)


def fused(count, grad_scale, nx, weights, cosine, sine, seg_q, seg_k, out_grads):
    total = nx.shape[0]
    own = total - W
    half = own // 2
    pairs = HALF // PAIR
    share = D // count
    chunks = 4
    whole = pl.BlockSpec(memory_space=pltpu.VMEM)

    def columns(start):
        return pl.BlockSpec((D, PAIR), lambda p: (0, start + p))

    bf16, f32 = jnp.bfloat16, jnp.float32
    return pl.pallas_call(
        functools.partial(fused_kernel, count=count, grad_scale=grad_scale),
        out_shape=[
            jax.ShapeDtypeStruct((half, D), bf16),
            jax.ShapeDtypeStruct((half, D), f32),
            jax.ShapeDtypeStruct((share, 3 * D), f32),
        ],
        grid=(pairs,),
        in_specs=[
            whole, columns(0), columns(pairs), columns(2 * pairs), whole, whole, whole, whole,
            pl.BlockSpec((own, PAIR), lambda p: (0, p)),
        ],
        out_specs=[whole, whole, whole],
        scratch_shapes=[
            pltpu.VMEM((own // BLOCK, BLOCK, SPAN), f32),
            pltpu.VMEM((own, PAIR), bf16),
            pltpu.VMEM((total, PAIR), bf16),
            pltpu.VMEM((total, PAIR), bf16),
            pltpu.VMEM((total, PAIR), f32),
            pltpu.VMEM((total, PAIR), f32),
            pltpu.VMEM((own, PAIR), bf16),
            pltpu.VMEM((total, 2 * PAIR), bf16),
            pltpu.VMEM((pairs, own, PAIR), bf16),
            pltpu.VMEM((pairs, half, PAIR), bf16),
            pltpu.VMEM((total, D), f32),
            pltpu.VMEM((pairs, D, 3 * PAIR), bf16),
            pltpu.VMEM((pairs, count - 1, share, 3 * PAIR), bf16),
            pltpu.VMEM((chunks, half // chunks, D), bf16),
            pltpu.VMEM((chunks, half // chunks, D), bf16),
            pltpu.VMEM((half, D), bf16),
            pltpu.VMEM((half, D), bf16),
            pltpu.VMEM((chunks, half // chunks, D), bf16),
            pltpu.VMEM((chunks, half // chunks, D), bf16),
            pltpu.SemaphoreType.DMA((pairs, count - 1)),
            pltpu.SemaphoreType.DMA((pairs, count - 1)),
            pltpu.SemaphoreType.DMA((pairs,)),
            pltpu.SemaphoreType.DMA((pairs,)),
            pltpu.SemaphoreType.DMA((chunks + 1,)),
            pltpu.SemaphoreType.DMA((chunks + 1,)),
            pltpu.SemaphoreType.DMA((chunks,)),
            pltpu.SemaphoreType.DMA((chunks,)),
        ],
        compiler_params=pltpu.CompilerParams(
            vmem_limit_bytes=56 * 1024 * 1024, collective_id=0, has_side_effects=True
        ),
        name="fused_attention",
    )(nx, weights, weights, weights, cosine, sine, seg_q, seg_k, out_grads)


def own_columns(weights, core):
    return jnp.concatenate(
        [lax.dynamic_slice_in_dim(weights, t * D + core * HALF, HALF, 1) for t in range(3)], axis=1
    )


def swapped(value):
    count = lax.axis_size("seq")
    return lax.ppermute(value, "seq", [(s, s ^ 1) for s in range(count)])


def chip_shifted(value, steps):
    count = lax.axis_size("seq")
    pairs = [(s, s + 2 * steps) for s in range(count) if 0 <= s + 2 * steps < count]
    return lax.ppermute(value, "seq", pairs)


def ordered(core, mine, other, axis=0):
    first = jnp.where(core == 0, mine, other)
    second = jnp.where(core == 0, other, mine)
    return jnp.concatenate([first, second], axis=axis)


def local(inputs, projection, positions, segments, context_grad):
    row_count = inputs.shape[0]
    device_count = lax.axis_size("seq")
    chips = device_count // 2
    device_index = lax.axis_index("seq")
    core = device_index % 2
    chip = device_index // 2
    assert 2 * row_count == W
    grad_scale = (row_count * device_count) ** (-0.5)

    weights = lax.all_gather(projection, "seq", axis=0, tiled=True)

    meta = jnp.stack([positions, segments], axis=0)
    x_before = chip_shifted(inputs, 1)
    meta_before = chip_shifted(meta, 1)
    x_other = swapped(inputs)
    meta_other = swapped(meta)
    x_before_other = swapped(x_before)
    meta_before_other = swapped(meta_before)
    grad_mine = lax.dynamic_slice_in_dim(context_grad, core * HALF, HALF, 1)
    grad_sent = lax.dynamic_slice_in_dim(context_grad, (1 - core) * HALF, HALF, 1)
    grad_other = swapped(grad_sent)
    out_grads = ordered(core, grad_mine, grad_other)

    x_all = jnp.concatenate(
        [ordered(core, x_before, x_before_other), ordered(core, inputs, x_other)], axis=0
    ).astype(jnp.float32)
    nx = (
        x_all * lax.rsqrt(jnp.mean(x_all * x_all, axis=1, keepdims=True) + EPSILON)
    ).astype(jnp.bfloat16)
    meta_all = jnp.concatenate(
        [ordered(core, meta_before, meta_before_other, 1), ordered(core, meta, meta_other, 1)],
        axis=1,
    )
    half_size = HD // 2
    frequency = jnp.exp(-math.log(10000.0) * jnp.arange(half_size, dtype=jnp.float32) / half_size)
    angle = meta_all[0].astype(jnp.float32)[:, None] * frequency[None, :]
    c, s = jnp.cos(angle), jnp.sin(angle)
    cosine = jnp.concatenate([c, c, c, c], axis=1)
    sine = jnp.concatenate([-s, s, -s, s], axis=1)
    seg_all = meta_all[1]
    outside = (jnp.arange(seg_all.shape[0]) < W) & (chip == 0)
    seg_k = jnp.where(outside, -1, seg_all)[None, :]
    seg_q = seg_all[W:][:, None]

    x_float = inputs.astype(jnp.float32)
    inv_rms = lax.rsqrt(jnp.mean(x_float * x_float, axis=1, keepdims=True) + EPSILON)
    scaled = x_float * inv_rms

    if (D // device_count) % 16 == 0:
        context, normed_grad, projection_grad = fused(
            device_count, grad_scale, nx, own_columns(weights, core), cosine, sine, seg_q, seg_k,
            out_grads,
        )
        input_grad = (
            inv_rms * (normed_grad - scaled * jnp.mean(normed_grad * scaled, axis=1, keepdims=True))
        ).astype(jnp.bfloat16)
        return (context, input_grad, projection_grad)

    context_heads, dq, dk, dv = attention(
        core.astype(jnp.int32)[None], nx, weights, cosine, sine, seg_q, seg_k, out_grads
    )

    mine_at = core * row_count
    other_at = (1 - core) * row_count
    context_mine = lax.dynamic_slice_in_dim(context_heads, mine_at, row_count, 0)
    context_other = swapped(lax.dynamic_slice_in_dim(context_heads, other_at, row_count, 0))
    context = ordered(core, context_mine, context_other, 1)

    w_q, w_k, w_v = [
        lax.dynamic_slice_in_dim(weights, t * D + core * HALF, HALF, 1) for t in range(3)
    ]
    dkv = jnp.concatenate([dk, dv], axis=1)
    w_kv = jnp.concatenate([w_k, w_v], axis=1)
    ng_kv = contract(dkv, w_kv, 1, 1)
    ng_q = contract(dq, w_q, 1, 1)
    ng_before = ng_kv[:W]
    ng_own = ng_kv[W:] + ng_q
    send_before = lax.dynamic_slice_in_dim(ng_before, other_at, row_count, 0).astype(jnp.bfloat16)
    keep_before = lax.dynamic_slice_in_dim(ng_before, mine_at, row_count, 0)
    before = keep_before + swapped(send_before).astype(jnp.float32)
    later = chip_shifted(before.astype(jnp.bfloat16), -1)
    send_own = lax.dynamic_slice_in_dim(ng_own, other_at, row_count, 0).astype(jnp.bfloat16)
    keep_own = lax.dynamic_slice_in_dim(ng_own, mine_at, row_count, 0)
    normed_grad = (
        keep_own + swapped(send_own).astype(jnp.float32) + later.astype(jnp.float32)
    )
    input_grad = (
        inv_rms * (normed_grad - scaled * jnp.mean(normed_grad * scaled, axis=1, keepdims=True))
    ).astype(jnp.bfloat16)

    pg_kv = contract(nx, dkv, 0, 0)
    pg_q = contract(nx[W:], dq, 0, 0)
    pg = jnp.concatenate([pg_q, pg_kv], axis=1).astype(jnp.bfloat16)
    groups = [[2 * i + k for i in range(chips)] for k in range(2)]
    summed = lax.psum_scatter(
        pg, "seq", scatter_dimension=0, axis_index_groups=groups, tiled=True
    ).astype(jnp.float32)
    rows = summed.shape[0] // 2
    keep = lax.dynamic_slice_in_dim(summed, core * rows, rows, 0)
    other = swapped(lax.dynamic_slice_in_dim(summed, (1 - core) * rows, rows, 0).astype(jnp.bfloat16))
    other = other.astype(jnp.float32)
    parts = []
    for t in range(3):
        cols = slice(t * HALF, (t + 1) * HALF)
        parts.append(ordered(core, keep[:, cols], other[:, cols], 1))
    projection_grad = jnp.concatenate(parts, axis=1) * grad_scale
    return (context, input_grad, projection_grad)


def solution(mesh):
    in_specs = (
        P(("groups", "seq"), None),
        P("seq", None),
        P(("groups", "seq")),
        P(("groups", "seq")),
        P(("groups", "seq"), None),
    )
    out_specs = (P(("groups", "seq"), None), P(("groups", "seq"), None), P(("groups", "seq"), None))
    return jax.shard_map(local, mesh=mesh, in_specs=in_specs, out_specs=out_specs, check_vma=False)
```

```python
import functools
import math

import jax
import jax.numpy as jnp
from jax import lax
from jax.experimental import pallas as pl
from jax.experimental.pallas import tpu as pltpu
from jax.sharding import PartitionSpec as P

D = 768
H = 12
HD = 64
W = 1024
EPSILON = 1e-05
SCORE_SCALE = 0.125
MASKED_SCORE = -1e30
BLOCK = 256
SPAN = BLOCK + W
PAIR = 2 * HD
HALF = D // 2


def contract(a, b, da, db):
    return lax.dot_general(a, b, (((da,), (db,)), ((), ())), preferred_element_type=jnp.float32)


def swap_halves(u, lane):
    low = (lane % HD) < HD // 2
    return jnp.where(low, pltpu.roll(u, PAIR - HD // 2, 1), pltpu.roll(u, HD // 2, 1))


def fill_bias(bias, segq_ref, segk_ref):
    row = lax.broadcasted_iota(jnp.int32, (BLOCK, SPAN), 0)
    col = lax.broadcasted_iota(jnp.int32, (BLOCK, SPAN), 1)
    near = (col > row) & (col <= row + W)
    for b in range(bias.shape[0]):
        same = segq_ref[b * BLOCK : (b + 1) * BLOCK, :] == segk_ref[:, b * BLOCK : b * BLOCK + SPAN]
        bias[b] = jnp.where(near & same, 0.0, MASKED_SCORE)


def pair_attention(
    nx_ref, wq_ref, wk_ref, wv_ref, cos_ref, sin_ref, do_ref,
    ctx_ref, dq_ref,
    bias, qs, ks, vs, dka, dva,
):
    own = ctx_ref.shape[0]
    total = nx_ref.shape[0]
    lane = lax.broadcasted_iota(jnp.int32, (1, PAIR), 1)

    def swap(u):
        return swap_halves(u, lane)

    def project(i, carry):
        rows = pl.ds(pl.multiple_of(i * BLOCK, BLOCK), BLOCK)
        x = nx_ref[rows, :]
        k = contract(x, wk_ref[...], 1, 0)
        ks[rows, :] = (k * cos_ref[rows, :] + swap(k) * sin_ref[rows, :]).astype(jnp.bfloat16)
        vs[rows, :] = contract(x, wv_ref[...], 1, 0).astype(jnp.bfloat16)
        dka[rows, :] = jnp.zeros((BLOCK, PAIR), jnp.float32)
        dva[rows, :] = jnp.zeros((BLOCK, PAIR), jnp.float32)
        return carry

    lax.fori_loop(0, total // BLOCK, project, 0)

    def query(i, carry):
        rows = pl.ds(pl.multiple_of(i * BLOCK, BLOCK), BLOCK)
        here = pl.ds(pl.multiple_of(i * BLOCK + W, BLOCK), BLOCK)
        q = contract(nx_ref[here, :], wq_ref[...], 1, 0)
        q = (q * cos_ref[here, :] + swap(q) * sin_ref[here, :]).astype(jnp.bfloat16)
        qs[rows, :] = q * jnp.bfloat16(SCORE_SCALE)
        return carry

    lax.fori_loop(0, own // BLOCK, query, 0)

    def visit(b, carry):
        rows = pl.ds(pl.multiple_of(b * BLOCK, BLOCK), BLOCK)
        here = pl.ds(pl.multiple_of(b * BLOCK + W, BLOCK), BLOCK)
        window = pl.ds(pl.multiple_of(b * BLOCK, BLOCK), SPAN)
        contexts, grads, keep = [], [], []
        for h in range(2):
            mine = (lane // HD) == h
            kb = ks[window, :]
            vb = vs[window, :]
            qh = jnp.where(mine, qs[rows, :], jnp.bfloat16(0))
            gh = jnp.where(mine, do_ref[rows, :], jnp.bfloat16(0))
            s = contract(qh, kb, 1, 1) + bias[b]
            e = jnp.exp(s - jnp.max(s, axis=1, keepdims=True))
            w = e * (1.0 / jnp.sum(e, axis=1, keepdims=True))
            pb = w.astype(jnp.bfloat16)
            context = contract(pb, vb, 1, 0).astype(jnp.bfloat16)
            delta = jnp.sum(
                gh.astype(jnp.float32) * context.astype(jnp.float32), axis=1, keepdims=True
            )
            dp = contract(gh, vb, 1, 1)
            ds = (w * (dp - delta)).astype(jnp.bfloat16)
            contexts.append(context)
            grads.append(contract(ds, kb, 1, 0))
            keep.append((ds, qh, pb, gh))
        ds, qh, pb, gh = [
            jnp.concatenate([keep[0][n], keep[1][n]], axis=0) for n in range(4)
        ]
        dka[window, :] += contract(qh, ds, 0, 0).T
        dva[window, :] += contract(gh, pb, 0, 0).T
        first = lane < HD
        ctx_ref[rows, :] = jnp.where(first, contexts[0], contexts[1])
        g = jnp.where(first, grads[0], grads[1]) * SCORE_SCALE
        dq_ref[rows, :] = (g * cos_ref[here, :] - swap(g) * sin_ref[here, :]).astype(jnp.bfloat16)
        return carry

    lax.fori_loop(0, own // BLOCK, visit, 0, unroll=2)


def attention_kernel(
    core_ref, nx_ref, wq_ref, wk_ref, wv_ref, cos_ref, sin_ref, segq_ref, segk_ref, do_ref,
    ctx_ref, dq_ref, dk_ref, dv_ref,
    bias, qs, ks, vs, dka, dva,
):
    total = nx_ref.shape[0]
    lane = lax.broadcasted_iota(jnp.int32, (1, PAIR), 1)

    def swap(u):
        return swap_halves(u, lane)

    @pl.when(pl.program_id(0) == 0)
    def _():
        fill_bias(bias, segq_ref, segk_ref)

    pair_attention(
        nx_ref, wq_ref, wk_ref, wv_ref, cos_ref, sin_ref, do_ref, ctx_ref, dq_ref, bias, qs, ks, vs, dka, dva,
    )

    def finish(i, carry):
        rows = pl.ds(pl.multiple_of(i * BLOCK, BLOCK), BLOCK)
        g = dka[rows, :]
        dk_ref[rows, :] = (g * cos_ref[rows, :] - swap(g) * sin_ref[rows, :]).astype(jnp.bfloat16)
        dv_ref[rows, :] = dva[rows, :].astype(jnp.bfloat16)
        return carry

    lax.fori_loop(0, total // BLOCK, finish, 0)


def attention(core, nx, weights, cosine, sine, seg_q, seg_k, out_grads):
    total = nx.shape[0]
    own = total - W
    pairs = HALF // PAIR

    def whole(shape):
        return pl.BlockSpec(shape, lambda p, c: (0, 0))

    def columns(start):
        return pl.BlockSpec((D, PAIR), lambda p, c: (0, start + c[0] * pairs + p))

    def heads(rows):
        return pl.BlockSpec((rows, PAIR), lambda p, c: (0, p))

    return pl.pallas_call(
        attention_kernel,
        out_shape=[
            jax.ShapeDtypeStruct((own, HALF), jnp.bfloat16),
            jax.ShapeDtypeStruct((own, HALF), jnp.bfloat16),
            jax.ShapeDtypeStruct((total, HALF), jnp.bfloat16),
            jax.ShapeDtypeStruct((total, HALF), jnp.bfloat16),
        ],
        grid_spec=pltpu.PrefetchScalarGridSpec(
            num_scalar_prefetch=1,
            grid=(pairs,),
            in_specs=[
                whole((total, D)),
                columns(0),
                columns(2 * pairs),
                columns(4 * pairs),
                whole((total, PAIR)),
                whole((total, PAIR)),
                whole((own, 1)),
                whole((1, total)),
                heads(own),
            ],
            out_specs=[heads(own), heads(own), heads(total), heads(total)],
            scratch_shapes=[
                pltpu.VMEM((own // BLOCK, BLOCK, SPAN), jnp.float32),
                pltpu.VMEM((own, PAIR), jnp.bfloat16),
                pltpu.VMEM((total, PAIR), jnp.bfloat16),
                pltpu.VMEM((total, PAIR), jnp.bfloat16),
                pltpu.VMEM((total, PAIR), jnp.float32),
                pltpu.VMEM((total, PAIR), jnp.float32),
            ],
        ),
        compiler_params=pltpu.CompilerParams(vmem_limit_bytes=48 * 1024 * 1024),
        name="window_attention",
    )(core, nx, weights, weights, weights, cosine, sine, seg_q, seg_k, out_grads)


def fused_kernel(
    own_ref, wl_ref, cos_ref, sin_ref, segq_ref, segk_ref, cg_ref,
    ctx_ref, ng_ref, pg_ref,
    nx_ref, wbuf, gbuf, w_send, w_recv, n_send, n_recv, g_send, g_recv,
    bias, qs, ks, vs, dka, dva, dqs, dkv, ctxs, ctxr, acc, part, sums, xs, xr, ys, yr, fwd, later,
    part_send, part_recv, ctx_send, ctx_recv, x_send, x_recv, fwd_send, fwd_recv,
    *, count, grad_scale,
):
    p = pl.program_id(0)
    last = pl.num_programs(0) - 1
    me = lax.axis_index("seq")
    core = lax.rem(me, 2)
    partner = me + 1 - 2 * core
    total = nx_ref.shape[0]
    own = total - W
    half = own // 2
    share = D // count
    chunks = xs.shape[0]
    piece = half // chunks
    wq_ref = wbuf.at[p, :, :PAIR]
    wk_ref = wbuf.at[p, :, PAIR : 2 * PAIR]
    wv_ref = wbuf.at[p, :, 2 * PAIR :]
    my_rows = pl.ds(pl.multiple_of(me * share, share), share)
    mine_at = pl.multiple_of(core * half, half)
    other_at = pl.multiple_of((1 - core) * half, half)

    def remote(source, target, send, recv, device):
        return pltpu.make_async_remote_copy(
            src_ref=source, dst_ref=target, send_sem=send, recv_sem=recv,
            device_id={"seq": device}, device_id_type=pl.DeviceIdType.MESH,
        )

    @pl.when(p == 0)
    def _():
        barrier = pltpu.get_barrier_semaphore()

        def greet(i, carry):
            pl.semaphore_signal(
                barrier, inc=1, device_id={"seq": lax.rem(me + 1 + i, count)},
                device_id_type=pl.DeviceIdType.MESH,
            )
            return carry

        lax.fori_loop(0, count - 1, greet, 0)
        pl.semaphore_wait(barrier, count - 1)

    def w_copy(pair, i):
        target = lax.rem(me + 1 + i, count)
        return remote(
            wl_ref.at[lax.rem(target, 2), pair], wbuf.at[pair, my_rows, :],
            w_send.at[pair, i], w_recv.at[pair, i], target,
        )

    def send_weights(pair):
        def start(i, carry):
            w_copy(pair, i).start()
            return carry

        lax.fori_loop(0, count - 1, start, 0)

    def g_copy(pair):
        cols = pl.ds(pl.multiple_of((1 - core) * HALF + pair * PAIR, PAIR), PAIR)
        return remote(
            cg_ref.at[:, cols], gbuf.at[pair, pl.ds(mine_at, half), :],
            g_send.at[pair], g_recv.at[pair], partner,
        )

    def partner_copy():
        return remote(
            own_ref, nx_ref.at[pl.ds(W + mine_at, half), :], n_send.at[0], n_recv.at[0], partner
        )

    def halo_copy():
        return remote(
            own_ref, nx_ref.at[pl.ds(mine_at, half), :], n_send.at[1], n_recv.at[1],
            lax.rem(me + 2, count),
        )

    def relay_copy():
        rows = pl.ds(mine_at, half)
        return remote(nx_ref.at[rows, :], nx_ref.at[rows, :], n_send.at[2], n_recv.at[2], partner)

    @pl.when(p == 0)
    def _():
        @pl.when(me < count - 2)
        def _():
            halo_copy().start()

        send_weights(0)
        partner_copy().start()
        for pair in range(3):
            g_copy(pair).start()
        nx_ref[pl.ds(W + mine_at, half), :] = own_ref[...]
        for pair in range(3):
            wbuf[pair, my_rows, :] = wl_ref[core, pair]
            cols = pl.ds(pl.multiple_of(core * HALF + pair * PAIR, PAIR), PAIR)
            gbuf[pair, pl.ds(mine_at, half), :] = cg_ref[:, cols]

        @pl.when(me < 2)
        def _():
            nx_ref[:W, :] = jnp.zeros((W, D), jnp.bfloat16)

        fill_bias(bias, segq_ref, segk_ref)

        @pl.when(me >= 2)
        def _():
            halo_copy().wait_recv()
            relay_copy().start()

    def arrive_weights(i, carry):
        w_copy(p, i).wait()
        return carry

    lax.fori_loop(0, count - 1, arrive_weights, 0)
    g_copy(p).wait()

    @pl.when(p == 0)
    def _():
        send_weights(1)
        send_weights(2)
        partner_copy().wait()

        @pl.when(me >= 2)
        def _():
            relay_copy().wait()

        @pl.when(me < count - 2)
        def _():
            halo_copy().wait_send()

    pair_attention(
        nx_ref, wq_ref, wk_ref, wv_ref, cos_ref, sin_ref, gbuf.at[p],
        ctxs.at[p], dqs, bias, qs, ks, vs, dka, dva,
    )

    def ctx_copy(pair):
        return remote(
            ctxs.at[pair, pl.ds(other_at, half), :], ctxr.at[pair],
            ctx_send.at[pair], ctx_recv.at[pair], partner,
        )

    ctx_copy(p).start()

    lane = lax.broadcasted_iota(jnp.int32, (1, PAIR), 1)
    wkv = jnp.concatenate([wk_ref[...], wv_ref[...]], axis=1)

    def finish(i, carry):
        rows = pl.ds(pl.multiple_of(i * BLOCK, BLOCK), BLOCK)
        g = dka[rows, :]
        dk = (g * cos_ref[rows, :] - swap_halves(g, lane) * sin_ref[rows, :]).astype(jnp.bfloat16)
        block = jnp.concatenate([dk, dva[rows, :].astype(jnp.bfloat16)], axis=1)
        dkv[rows, :] = block
        grown = contract(block, wkv, 1, 1)

        @pl.when(p == 0)
        def _():
            acc[rows, :] = grown

        @pl.when(p > 0)
        def _():
            acc[rows, :] += grown

        return carry

    lax.fori_loop(0, total // BLOCK, finish, 0)

    def finish_query(i, carry):
        rows = pl.ds(pl.multiple_of(i * BLOCK, BLOCK), BLOCK)
        here = pl.ds(pl.multiple_of(i * BLOCK + W, BLOCK), BLOCK)
        acc[here, :] += contract(dqs[rows, :], wq_ref[...], 1, 1)
        return carry

    lax.fori_loop(0, own // BLOCK, finish_query, 0)

    def x_copy(j):
        return remote(xs.at[j], xr.at[j], x_send.at[j], x_recv.at[j], partner)

    def own_copy():
        return remote(
            ys, yr, x_send.at[chunks], x_recv.at[chunks], partner
        )

    @pl.when(p == last)
    def _():
        for j in range(chunks):
            xs[j] = acc[pl.ds(other_at + j * piece, piece), :].astype(jnp.bfloat16)
            x_copy(j).start()
        ys[...] = acc[pl.ds(W + other_at, half), :].astype(jnp.bfloat16)
        own_copy().start()

    def project_grad(j, carry):
        cols = pl.ds(pl.multiple_of(j * BLOCK, BLOCK), BLOCK)
        part[p, cols, :PAIR] = contract(nx_ref[W:, cols], dqs[...], 0, 0).astype(jnp.bfloat16)
        part[p, cols, PAIR:] = contract(nx_ref[:, cols], dkv[...], 0, 0).astype(jnp.bfloat16)
        return carry

    lax.fori_loop(0, D // BLOCK, project_grad, 0)

    def fwd_copy(j):
        return remote(fwd.at[j], later.at[j], fwd_send.at[j], fwd_recv.at[j], lax.rem(me + count - 2, count))

    @pl.when(p == last)
    def _():
        for j in range(chunks):
            x_copy(j).wait_recv()
            mine = acc[pl.ds(mine_at + j * piece, piece), :]
            fwd[j] = (mine + xr[j].astype(jnp.float32)).astype(jnp.bfloat16)

            @pl.when(me >= 2)
            def _():
                fwd_copy(j).start()

    def part_copy(pair, i):
        target = lax.rem(me + 1 + i, count)
        return remote(
            part.at[pair, pl.ds(pl.multiple_of(target * share, share), share), :],
            sums.at[pair, i], part_send.at[pair, i], part_recv.at[pair, i], target,
        )

    def send_part(i, carry):
        part_copy(p, i).start()
        return carry

    lax.fori_loop(0, count - 1, send_part, 0)

    @pl.when(p == last)
    def _():
        for pair in range(3):
            ctx_copy(pair).wait()
            mine_cols = pl.ds(pl.multiple_of(core * HALF + pair * PAIR, PAIR), PAIR)
            other_cols = pl.ds(pl.multiple_of((1 - core) * HALF + pair * PAIR, PAIR), PAIR)
            ctx_ref[:, mine_cols] = ctxs[pair, pl.ds(mine_at, half), :]
            ctx_ref[:, other_cols] = ctxr[pair]

        def sum_pair(pair):
            def arrive(i, carry):
                part_copy(pair, i).wait()
                return carry

            lax.fori_loop(0, count - 1, arrive, 0)

            def add(i, carry):
                odd, even = carry
                return (
                    odd + sums[pair, 2 * i].astype(jnp.float32),
                    even + sums[pair, 2 * i + 1].astype(jnp.float32),
                )

            kept = part[pair, pl.ds(pl.multiple_of(me * share, share), share), :]
            odd, even = lax.fori_loop(
                0, count // 2 - 1, add,
                (jnp.zeros((share, 3 * PAIR), jnp.float32), kept.astype(jnp.float32)),
            )
            odd = odd + sums[pair, count - 2].astype(jnp.float32)
            for t in range(3):
                at = t * D + pair * PAIR
                a = pl.ds(pl.multiple_of(at + core * HALF, PAIR), PAIR)
                b = pl.ds(pl.multiple_of(at + (1 - core) * HALF, PAIR), PAIR)
                pg_ref[:, a] = even[:, t * PAIR : (t + 1) * PAIR] * grad_scale
                pg_ref[:, b] = odd[:, t * PAIR : (t + 1) * PAIR] * grad_scale

        sum_pair(0)
        sum_pair(1)
        own_copy().wait()
        for j in range(chunks):
            x_copy(j).wait_send()
        ng_ref[...] = acc[pl.ds(W + mine_at, half), :] + yr[...].astype(jnp.float32)
        sum_pair(2)
        for j in range(chunks):

            @pl.when(me >= 2)
            def _():
                fwd_copy(j).wait_send()

            @pl.when(me < count - 2)
            def _():
                fwd_copy(j).wait_recv()
                ng_ref[j * piece : (j + 1) * piece, :] += later[j].astype(jnp.float32)


def fused(count, grad_scale, nx, weights, cosine, sine, seg_q, seg_k, out_grads):
    half = nx.shape[0]
    own = 2 * half
    total = own + W
    pairs = HALF // PAIR
    share = D // count
    chunks = 4
    whole = pl.BlockSpec(memory_space=pltpu.VMEM)

    bf16, f32 = jnp.bfloat16, jnp.float32
    return pl.pallas_call(
        functools.partial(fused_kernel, count=count, grad_scale=grad_scale),
        out_shape=[
            jax.ShapeDtypeStruct((half, D), bf16),
            jax.ShapeDtypeStruct((half, D), f32),
            jax.ShapeDtypeStruct((share, 3 * D), f32),
        ],
        grid=(pairs,),
        in_specs=[whole] * 7,
        out_specs=[whole, whole, whole],
        scratch_shapes=[
            pltpu.VMEM((total, D), bf16),
            pltpu.VMEM((pairs, D, 3 * PAIR), bf16),
            pltpu.VMEM((pairs, own, PAIR), bf16),
            pltpu.SemaphoreType.DMA((pairs, count - 1)),
            pltpu.SemaphoreType.DMA((pairs, count - 1)),
            pltpu.SemaphoreType.DMA((3,)),
            pltpu.SemaphoreType.DMA((3,)),
            pltpu.SemaphoreType.DMA((pairs,)),
            pltpu.SemaphoreType.DMA((pairs,)),
            pltpu.VMEM((own // BLOCK, BLOCK, SPAN), f32),
            pltpu.VMEM((own, PAIR), bf16),
            pltpu.VMEM((total, PAIR), bf16),
            pltpu.VMEM((total, PAIR), bf16),
            pltpu.VMEM((total, PAIR), f32),
            pltpu.VMEM((total, PAIR), f32),
            pltpu.VMEM((own, PAIR), bf16),
            pltpu.VMEM((total, 2 * PAIR), bf16),
            pltpu.VMEM((pairs, own, PAIR), bf16),
            pltpu.VMEM((pairs, half, PAIR), bf16),
            pltpu.VMEM((total, D), f32),
            pltpu.VMEM((pairs, D, 3 * PAIR), bf16),
            pltpu.VMEM((pairs, count - 1, share, 3 * PAIR), bf16),
            pltpu.VMEM((chunks, half // chunks, D), bf16),
            pltpu.VMEM((chunks, half // chunks, D), bf16),
            pltpu.VMEM((half, D), bf16),
            pltpu.VMEM((half, D), bf16),
            pltpu.VMEM((chunks, half // chunks, D), bf16),
            pltpu.VMEM((chunks, half // chunks, D), bf16),
            pltpu.SemaphoreType.DMA((pairs, count - 1)),
            pltpu.SemaphoreType.DMA((pairs, count - 1)),
            pltpu.SemaphoreType.DMA((pairs,)),
            pltpu.SemaphoreType.DMA((pairs,)),
            pltpu.SemaphoreType.DMA((chunks + 1,)),
            pltpu.SemaphoreType.DMA((chunks + 1,)),
            pltpu.SemaphoreType.DMA((chunks,)),
            pltpu.SemaphoreType.DMA((chunks,)),
        ],
        compiler_params=pltpu.CompilerParams(
            vmem_limit_bytes=56 * 1024 * 1024, collective_id=0, has_side_effects=True
        ),
        name="fused_attention",
    )(nx, weights, cosine, sine, seg_q, seg_k, out_grads)


def tables(meta_all, chip):
    half_size = HD // 2
    frequency = jnp.exp(-math.log(10000.0) * jnp.arange(half_size, dtype=jnp.float32) / half_size)
    angle = meta_all[0].astype(jnp.float32)[:, None] * frequency[None, :]
    c, s = jnp.cos(angle), jnp.sin(angle)
    cosine = jnp.concatenate([c, c, c, c], axis=1)
    sine = jnp.concatenate([-s, s, -s, s], axis=1)
    seg_all = meta_all[1]
    outside = (jnp.arange(seg_all.shape[0]) < W) & (chip == 0)
    seg_k = jnp.where(outside, -1, seg_all)[None, :]
    seg_q = seg_all[W:][:, None]
    return cosine, sine, seg_q, seg_k


def swapped(value):
    count = lax.axis_size("seq")
    return lax.ppermute(value, "seq", [(s, s ^ 1) for s in range(count)])


def chip_shifted(value, steps):
    count = lax.axis_size("seq")
    pairs = [(s, s + 2 * steps) for s in range(count) if 0 <= s + 2 * steps < count]
    return lax.ppermute(value, "seq", pairs)


def ordered(core, mine, other, axis=0):
    first = jnp.where(core == 0, mine, other)
    second = jnp.where(core == 0, other, mine)
    return jnp.concatenate([first, second], axis=axis)


def local(inputs, projection, positions, segments, context_grad):
    row_count = inputs.shape[0]
    device_count = lax.axis_size("seq")
    chips = device_count // 2
    device_index = lax.axis_index("seq")
    core = device_index % 2
    chip = device_index // 2
    assert 2 * row_count == W
    grad_scale = (row_count * device_count) ** (-0.5)

    meta = jnp.stack([positions, segments], axis=0)
    x_float = inputs.astype(jnp.float32)
    inv_rms = lax.rsqrt(jnp.mean(x_float * x_float, axis=1, keepdims=True) + EPSILON)
    scaled = x_float * inv_rms

    if (D // device_count) % 16 == 0:
        crossed = [(s, (s + 2) ^ 1) for s in range(device_count - 2)]
        meta_all = jnp.concatenate(
            [
                ordered(core, chip_shifted(meta, 1), lax.ppermute(meta, "seq", crossed), 1),
                ordered(core, meta, swapped(meta), 1),
            ],
            axis=1,
        )
        cosine, sine, seg_q, seg_k = tables(meta_all, chip)
        pieces = projection.reshape(D // device_count, 3, 2, 3, PAIR)
        pieces = jnp.transpose(pieces, (2, 3, 0, 1, 4)).reshape(2, 3, D // device_count, 3 * PAIR)
        context, normed_grad, projection_grad = fused(
            device_count, grad_scale, scaled.astype(jnp.bfloat16), pieces, cosine, sine, seg_q,
            seg_k, context_grad,
        )
        input_grad = (
            inv_rms * (normed_grad - scaled * jnp.mean(normed_grad * scaled, axis=1, keepdims=True))
        ).astype(jnp.bfloat16)
        return (context, input_grad, projection_grad)

    weights = lax.all_gather(projection, "seq", axis=0, tiled=True)
    x_before = chip_shifted(inputs, 1)
    meta_before = chip_shifted(meta, 1)
    x_other = swapped(inputs)
    meta_other = swapped(meta)
    x_before_other = swapped(x_before)
    meta_before_other = swapped(meta_before)
    grad_mine = lax.dynamic_slice_in_dim(context_grad, core * HALF, HALF, 1)
    grad_sent = lax.dynamic_slice_in_dim(context_grad, (1 - core) * HALF, HALF, 1)
    grad_other = swapped(grad_sent)
    out_grads = ordered(core, grad_mine, grad_other)

    x_all = jnp.concatenate(
        [ordered(core, x_before, x_before_other), ordered(core, inputs, x_other)], axis=0
    ).astype(jnp.float32)
    nx = (
        x_all * lax.rsqrt(jnp.mean(x_all * x_all, axis=1, keepdims=True) + EPSILON)
    ).astype(jnp.bfloat16)
    meta_all = jnp.concatenate(
        [ordered(core, meta_before, meta_before_other, 1), ordered(core, meta, meta_other, 1)],
        axis=1,
    )
    cosine, sine, seg_q, seg_k = tables(meta_all, chip)
    context_heads, dq, dk, dv = attention(
        core.astype(jnp.int32)[None], nx, weights, cosine, sine, seg_q, seg_k, out_grads
    )

    mine_at = core * row_count
    other_at = (1 - core) * row_count
    context_mine = lax.dynamic_slice_in_dim(context_heads, mine_at, row_count, 0)
    context_other = swapped(lax.dynamic_slice_in_dim(context_heads, other_at, row_count, 0))
    context = ordered(core, context_mine, context_other, 1)

    w_q, w_k, w_v = [
        lax.dynamic_slice_in_dim(weights, t * D + core * HALF, HALF, 1) for t in range(3)
    ]
    dkv = jnp.concatenate([dk, dv], axis=1)
    w_kv = jnp.concatenate([w_k, w_v], axis=1)
    ng_kv = contract(dkv, w_kv, 1, 1)
    ng_q = contract(dq, w_q, 1, 1)
    ng_before = ng_kv[:W]
    ng_own = ng_kv[W:] + ng_q
    send_before = lax.dynamic_slice_in_dim(ng_before, other_at, row_count, 0).astype(jnp.bfloat16)
    keep_before = lax.dynamic_slice_in_dim(ng_before, mine_at, row_count, 0)
    before = keep_before + swapped(send_before).astype(jnp.float32)
    later = chip_shifted(before.astype(jnp.bfloat16), -1)
    send_own = lax.dynamic_slice_in_dim(ng_own, other_at, row_count, 0).astype(jnp.bfloat16)
    keep_own = lax.dynamic_slice_in_dim(ng_own, mine_at, row_count, 0)
    normed_grad = (
        keep_own + swapped(send_own).astype(jnp.float32) + later.astype(jnp.float32)
    )
    input_grad = (
        inv_rms * (normed_grad - scaled * jnp.mean(normed_grad * scaled, axis=1, keepdims=True))
    ).astype(jnp.bfloat16)

    pg_kv = contract(nx, dkv, 0, 0)
    pg_q = contract(nx[W:], dq, 0, 0)
    pg = jnp.concatenate([pg_q, pg_kv], axis=1).astype(jnp.bfloat16)
    groups = [[2 * i + k for i in range(chips)] for k in range(2)]
    summed = lax.psum_scatter(
        pg, "seq", scatter_dimension=0, axis_index_groups=groups, tiled=True
    ).astype(jnp.float32)
    rows = summed.shape[0] // 2
    keep = lax.dynamic_slice_in_dim(summed, core * rows, rows, 0)
    other = swapped(lax.dynamic_slice_in_dim(summed, (1 - core) * rows, rows, 0).astype(jnp.bfloat16))
    other = other.astype(jnp.float32)
    parts = []
    for t in range(3):
        cols = slice(t * HALF, (t + 1) * HALF)
        parts.append(ordered(core, keep[:, cols], other[:, cols], 1))
    projection_grad = jnp.concatenate(parts, axis=1) * grad_scale
    return (context, input_grad, projection_grad)


def solution(mesh):
    in_specs = (
        P(("groups", "seq"), None),
        P("seq", None),
        P(("groups", "seq")),
        P(("groups", "seq")),
        P(("groups", "seq"), None),
    )
    out_specs = (P(("groups", "seq"), None), P(("groups", "seq"), None), P(("groups", "seq"), None))
    return jax.shard_map(local, mesh=mesh, in_specs=in_specs, out_specs=out_specs, check_vma=False)
```

```python
import functools
import math

import jax
import jax.numpy as jnp
from jax import lax
from jax.experimental import pallas as pl
from jax.experimental.pallas import tpu as pltpu
from jax.sharding import PartitionSpec as P

D = 768
H = 12
HD = 64
W = 1024
EPSILON = 1e-05
SCORE_SCALE = 0.125
MASKED_SCORE = -1e30
BLOCK = 256
SPAN = BLOCK + W
PAIR = 2 * HD
HALF = D // 2


def contract(a, b, da, db):
    return lax.dot_general(a, b, (((da,), (db,)), ((), ())), preferred_element_type=jnp.float32)


def swap_halves(u, lane):
    low = (lane % HD) < HD // 2
    return jnp.where(low, pltpu.roll(u, PAIR - HD // 2, 1), pltpu.roll(u, HD // 2, 1))


def fill_bias(bias, segq_ref, segk_ref):
    row = lax.broadcasted_iota(jnp.int32, (BLOCK, SPAN), 0)
    col = lax.broadcasted_iota(jnp.int32, (BLOCK, SPAN), 1)
    near = (col > row) & (col <= row + W)
    for b in range(bias.shape[0]):
        same = segq_ref[b * BLOCK : (b + 1) * BLOCK, :] == segk_ref[:, b * BLOCK : b * BLOCK + SPAN]
        bias[b] = jnp.where(near & same, 0.0, MASKED_SCORE)


def pair_attention(
    nx_ref, wq_ref, wk_ref, wv_ref, cos_ref, sin_ref, do_ref,
    ctx_ref, dq_ref,
    bias, qs, ks, vs, dka, dva,
):
    own = ctx_ref.shape[0]
    total = nx_ref.shape[0]
    lane = lax.broadcasted_iota(jnp.int32, (1, PAIR), 1)

    def swap(u):
        return swap_halves(u, lane)

    def project(i, carry):
        rows = pl.ds(pl.multiple_of(i * BLOCK, BLOCK), BLOCK)
        x = nx_ref[rows, :]
        k = contract(x, wk_ref[...], 1, 0)
        ks[rows, :] = (k * cos_ref[rows, :] + swap(k) * sin_ref[rows, :]).astype(jnp.bfloat16)
        vs[rows, :] = contract(x, wv_ref[...], 1, 0).astype(jnp.bfloat16)
        dka[rows, :] = jnp.zeros((BLOCK, PAIR), jnp.float32)
        dva[rows, :] = jnp.zeros((BLOCK, PAIR), jnp.float32)
        return carry

    lax.fori_loop(0, total // BLOCK, project, 0)

    def query(i, carry):
        rows = pl.ds(pl.multiple_of(i * BLOCK, BLOCK), BLOCK)
        here = pl.ds(pl.multiple_of(i * BLOCK + W, BLOCK), BLOCK)
        q = contract(nx_ref[here, :], wq_ref[...], 1, 0)
        q = (q * cos_ref[here, :] + swap(q) * sin_ref[here, :]).astype(jnp.bfloat16)
        qs[rows, :] = q * jnp.bfloat16(SCORE_SCALE)
        return carry

    lax.fori_loop(0, own // BLOCK, query, 0)

    def visit(b, carry):
        rows = pl.ds(pl.multiple_of(b * BLOCK, BLOCK), BLOCK)
        here = pl.ds(pl.multiple_of(b * BLOCK + W, BLOCK), BLOCK)
        window = pl.ds(pl.multiple_of(b * BLOCK, BLOCK), SPAN)
        contexts, grads, keep = [], [], []
        for h in range(2):
            mine = (lane // HD) == h
            kb = ks[window, :]
            vb = vs[window, :]
            qh = jnp.where(mine, qs[rows, :], jnp.bfloat16(0))
            gh = jnp.where(mine, do_ref[rows, :], jnp.bfloat16(0))
            s = contract(qh, kb, 1, 1) + bias[b]
            e = jnp.exp(s - jnp.max(s, axis=1, keepdims=True))
            w = e * (1.0 / jnp.sum(e, axis=1, keepdims=True))
            pb = w.astype(jnp.bfloat16)
            context = contract(pb, vb, 1, 0).astype(jnp.bfloat16)
            delta = jnp.sum(
                gh.astype(jnp.float32) * context.astype(jnp.float32), axis=1, keepdims=True
            )
            dp = contract(gh, vb, 1, 1)
            ds = (w * (dp - delta)).astype(jnp.bfloat16)
            contexts.append(context)
            grads.append(contract(ds, kb, 1, 0))
            keep.append((ds, qh, pb, gh))
        ds, qh, pb, gh = [
            jnp.concatenate([keep[0][n], keep[1][n]], axis=0) for n in range(4)
        ]
        dka[window, :] += contract(qh, ds, 0, 0).T
        dva[window, :] += contract(gh, pb, 0, 0).T
        first = lane < HD
        ctx_ref[rows, :] = jnp.where(first, contexts[0], contexts[1])
        g = jnp.where(first, grads[0], grads[1]) * SCORE_SCALE
        dq_ref[rows, :] = (g * cos_ref[here, :] - swap(g) * sin_ref[here, :]).astype(jnp.bfloat16)
        return carry

    lax.fori_loop(0, own // BLOCK, visit, 0, unroll=2)


def attention_kernel(
    core_ref, nx_ref, wq_ref, wk_ref, wv_ref, cos_ref, sin_ref, segq_ref, segk_ref, do_ref,
    ctx_ref, dq_ref, dk_ref, dv_ref,
    bias, qs, ks, vs, dka, dva,
):
    total = nx_ref.shape[0]
    lane = lax.broadcasted_iota(jnp.int32, (1, PAIR), 1)

    def swap(u):
        return swap_halves(u, lane)

    @pl.when(pl.program_id(0) == 0)
    def _():
        fill_bias(bias, segq_ref, segk_ref)

    pair_attention(
        nx_ref, wq_ref, wk_ref, wv_ref, cos_ref, sin_ref, do_ref, ctx_ref, dq_ref, bias, qs, ks, vs, dka, dva,
    )

    def finish(i, carry):
        rows = pl.ds(pl.multiple_of(i * BLOCK, BLOCK), BLOCK)
        g = dka[rows, :]
        dk_ref[rows, :] = (g * cos_ref[rows, :] - swap(g) * sin_ref[rows, :]).astype(jnp.bfloat16)
        dv_ref[rows, :] = dva[rows, :].astype(jnp.bfloat16)
        return carry

    lax.fori_loop(0, total // BLOCK, finish, 0)


def attention(core, nx, weights, cosine, sine, seg_q, seg_k, out_grads):
    total = nx.shape[0]
    own = total - W
    pairs = HALF // PAIR

    def whole(shape):
        return pl.BlockSpec(shape, lambda p, c: (0, 0))

    def columns(start):
        return pl.BlockSpec((D, PAIR), lambda p, c: (0, start + c[0] * pairs + p))

    def heads(rows):
        return pl.BlockSpec((rows, PAIR), lambda p, c: (0, p))

    return pl.pallas_call(
        attention_kernel,
        out_shape=[
            jax.ShapeDtypeStruct((own, HALF), jnp.bfloat16),
            jax.ShapeDtypeStruct((own, HALF), jnp.bfloat16),
            jax.ShapeDtypeStruct((total, HALF), jnp.bfloat16),
            jax.ShapeDtypeStruct((total, HALF), jnp.bfloat16),
        ],
        grid_spec=pltpu.PrefetchScalarGridSpec(
            num_scalar_prefetch=1,
            grid=(pairs,),
            in_specs=[
                whole((total, D)),
                columns(0),
                columns(2 * pairs),
                columns(4 * pairs),
                whole((total, PAIR)),
                whole((total, PAIR)),
                whole((own, 1)),
                whole((1, total)),
                heads(own),
            ],
            out_specs=[heads(own), heads(own), heads(total), heads(total)],
            scratch_shapes=[
                pltpu.VMEM((own // BLOCK, BLOCK, SPAN), jnp.float32),
                pltpu.VMEM((own, PAIR), jnp.bfloat16),
                pltpu.VMEM((total, PAIR), jnp.bfloat16),
                pltpu.VMEM((total, PAIR), jnp.bfloat16),
                pltpu.VMEM((total, PAIR), jnp.float32),
                pltpu.VMEM((total, PAIR), jnp.float32),
            ],
        ),
        compiler_params=pltpu.CompilerParams(vmem_limit_bytes=48 * 1024 * 1024),
        name="window_attention",
    )(core, nx, weights, weights, weights, cosine, sine, seg_q, seg_k, out_grads)


def fused_kernel(
    own_ref, wl_ref, cos_ref, sin_ref, segq_ref, segk_ref, cg_ref,
    ctx_ref, ng_ref, pg_ref,
    nx_ref, wbuf, gbuf, w_send, w_recv, n_send, n_recv, g_send, g_recv,
    bias, qs, ks, vs, dka, dva, dqs, dkv, ctxs, ctxr, acc, part, sums, xs, xr, ys, yr, fwd, later,
    part_send, part_recv, ctx_send, ctx_recv, x_send, x_recv, fwd_send, fwd_recv,
    *, count, grad_scale,
):
    p = pl.program_id(0)
    last = pl.num_programs(0) - 1
    me = lax.axis_index("seq")
    core = lax.rem(me, 2)
    partner = me + 1 - 2 * core
    total = nx_ref.shape[0]
    own = total - W
    half = own // 2
    share = D // count
    chunks = xs.shape[0]
    piece = half // chunks
    wq_ref = wbuf.at[p, :, :PAIR]
    wk_ref = wbuf.at[p, :, PAIR : 2 * PAIR]
    wv_ref = wbuf.at[p, :, 2 * PAIR :]
    my_rows = pl.ds(pl.multiple_of(me * share, share), share)
    mine_at = pl.multiple_of(core * half, half)
    other_at = pl.multiple_of((1 - core) * half, half)

    def remote(source, target, send, recv, device):
        return pltpu.make_async_remote_copy(
            src_ref=source, dst_ref=target, send_sem=send, recv_sem=recv,
            device_id={"seq": device}, device_id_type=pl.DeviceIdType.MESH,
        )

    @pl.when(p == 0)
    def _():
        barrier = pltpu.get_barrier_semaphore()

        def greet(i, carry):
            pl.semaphore_signal(
                barrier, inc=1, device_id={"seq": lax.rem(me + 1 + i, count)},
                device_id_type=pl.DeviceIdType.MESH,
            )
            return carry

        lax.fori_loop(0, count - 1, greet, 0)
        pl.semaphore_wait(barrier, count - 1)

    def w_copy(pair, i):
        target = lax.rem(me + 1 + i, count)
        return remote(
            wl_ref.at[lax.rem(target, 2), pair], wbuf.at[pair, my_rows, :],
            w_send.at[pair, i], w_recv.at[pair, i], target,
        )

    def send_weights(pair):
        def start(i, carry):
            w_copy(pair, i).start()
            return carry

        lax.fori_loop(0, count - 1, start, 0)

    def g_copy(pair):
        cols = pl.ds(pl.multiple_of((1 - core) * HALF + pair * PAIR, PAIR), PAIR)
        return remote(
            cg_ref.at[:, cols], gbuf.at[pair, pl.ds(mine_at, half), :],
            g_send.at[pair], g_recv.at[pair], partner,
        )

    def partner_copy():
        return remote(
            own_ref, nx_ref.at[pl.ds(W + mine_at, half), :], n_send.at[0], n_recv.at[0], partner
        )

    def halo_copy():
        return remote(
            own_ref, nx_ref.at[pl.ds(mine_at, half), :], n_send.at[1], n_recv.at[1],
            lax.rem(me + 2, count),
        )

    def relay_copy():
        rows = pl.ds(mine_at, half)
        return remote(nx_ref.at[rows, :], nx_ref.at[rows, :], n_send.at[2], n_recv.at[2], partner)

    @pl.when(p == 0)
    def _():
        @pl.when(me < count - 2)
        def _():
            halo_copy().start()

        send_weights(0)
        partner_copy().start()
        for pair in range(3):
            g_copy(pair).start()
        nx_ref[pl.ds(W + mine_at, half), :] = own_ref[...]
        for pair in range(3):
            wbuf[pair, my_rows, :] = wl_ref[core, pair]
            cols = pl.ds(pl.multiple_of(core * HALF + pair * PAIR, PAIR), PAIR)
            gbuf[pair, pl.ds(mine_at, half), :] = cg_ref[:, cols]

        @pl.when(me < 2)
        def _():
            nx_ref[:W, :] = jnp.zeros((W, D), jnp.bfloat16)

        fill_bias(bias, segq_ref, segk_ref)

        @pl.when(me >= 2)
        def _():
            halo_copy().wait_recv()
            relay_copy().start()

    def arrive_weights(i, carry):
        w_copy(p, i).wait()
        return carry

    lax.fori_loop(0, count - 1, arrive_weights, 0)
    g_copy(p).wait()

    @pl.when(p == 0)
    def _():
        send_weights(1)
        send_weights(2)
        partner_copy().wait()

        @pl.when(me >= 2)
        def _():
            relay_copy().wait()

        @pl.when(me < count - 2)
        def _():
            halo_copy().wait_send()

    pair_attention(
        nx_ref, wq_ref, wk_ref, wv_ref, cos_ref, sin_ref, gbuf.at[p],
        ctxs.at[p], dqs, bias, qs, ks, vs, dka, dva,
    )

    def ctx_copy(pair):
        return remote(
            ctxs.at[pair, pl.ds(other_at, half), :], ctxr.at[pair],
            ctx_send.at[pair], ctx_recv.at[pair], partner,
        )

    ctx_copy(p).start()

    lane = lax.broadcasted_iota(jnp.int32, (1, PAIR), 1)
    wkv = jnp.concatenate([wk_ref[...], wv_ref[...]], axis=1)

    def finish(i, carry):
        rows = pl.ds(pl.multiple_of(i * BLOCK, BLOCK), BLOCK)
        g = dka[rows, :]
        dk = (g * cos_ref[rows, :] - swap_halves(g, lane) * sin_ref[rows, :]).astype(jnp.bfloat16)
        block = jnp.concatenate([dk, dva[rows, :].astype(jnp.bfloat16)], axis=1)
        dkv[rows, :] = block
        grown = contract(block, wkv, 1, 1)

        @pl.when(p == 0)
        def _():
            acc[rows, :] = grown

        @pl.when(p > 0)
        def _():
            acc[rows, :] += grown

        return carry

    lax.fori_loop(0, W // BLOCK, finish, 0)

    def x_copy(j):
        return remote(xs.at[j], xr.at[j], x_send.at[j], x_recv.at[j], partner)

    def own_copy():
        return remote(
            ys, yr, x_send.at[chunks], x_recv.at[chunks], partner
        )

    @pl.when(p == last)
    def _():
        for j in range(chunks):
            xs[j] = acc[pl.ds(other_at + j * piece, piece), :].astype(jnp.bfloat16)
            x_copy(j).start()

    lax.fori_loop(W // BLOCK, total // BLOCK, finish, 0)

    def finish_query(i, carry):
        rows = pl.ds(pl.multiple_of(i * BLOCK, BLOCK), BLOCK)
        here = pl.ds(pl.multiple_of(i * BLOCK + W, BLOCK), BLOCK)
        acc[here, :] += contract(dqs[rows, :], wq_ref[...], 1, 1)
        return carry

    lax.fori_loop(0, own // BLOCK, finish_query, 0)

    @pl.when(p == last)
    def _():
        ys[...] = acc[pl.ds(W + other_at, half), :].astype(jnp.bfloat16)
        own_copy().start()

    def fwd_copy(j):
        return remote(fwd.at[j], later.at[j], fwd_send.at[j], fwd_recv.at[j], lax.rem(me + count - 2, count))

    @pl.when(p == last)
    def _():
        for j in range(chunks):
            x_copy(j).wait_recv()
            mine = acc[pl.ds(mine_at + j * piece, piece), :]
            fwd[j] = (mine + xr[j].astype(jnp.float32)).astype(jnp.bfloat16)

            @pl.when(me >= 2)
            def _():
                fwd_copy(j).start()

    def project_grad(j, carry):
        cols = pl.ds(pl.multiple_of(j * BLOCK, BLOCK), BLOCK)
        part[p, cols, :PAIR] = contract(nx_ref[W:, cols], dqs[...], 0, 0).astype(jnp.bfloat16)
        part[p, cols, PAIR:] = contract(nx_ref[:, cols], dkv[...], 0, 0).astype(jnp.bfloat16)
        return carry

    lax.fori_loop(0, D // BLOCK, project_grad, 0)

    def part_copy(pair, i):
        target = lax.rem(me + 1 + i, count)
        return remote(
            part.at[pair, pl.ds(pl.multiple_of(target * share, share), share), :],
            sums.at[pair, i], part_send.at[pair, i], part_recv.at[pair, i], target,
        )

    def send_part(i, carry):
        part_copy(p, i).start()
        return carry

    lax.fori_loop(0, count - 1, send_part, 0)

    @pl.when(p == last)
    def _():
        for pair in range(3):
            ctx_copy(pair).wait()
            mine_cols = pl.ds(pl.multiple_of(core * HALF + pair * PAIR, PAIR), PAIR)
            other_cols = pl.ds(pl.multiple_of((1 - core) * HALF + pair * PAIR, PAIR), PAIR)
            ctx_ref[:, mine_cols] = ctxs[pair, pl.ds(mine_at, half), :]
            ctx_ref[:, other_cols] = ctxr[pair]

        def sum_pair(pair):
            def arrive(i, carry):
                part_copy(pair, i).wait()
                return carry

            lax.fori_loop(0, count - 1, arrive, 0)

            def add(i, carry):
                odd, even = carry
                return (
                    odd + sums[pair, 2 * i].astype(jnp.float32),
                    even + sums[pair, 2 * i + 1].astype(jnp.float32),
                )

            kept = part[pair, pl.ds(pl.multiple_of(me * share, share), share), :]
            odd, even = lax.fori_loop(
                0, count // 2 - 1, add,
                (jnp.zeros((share, 3 * PAIR), jnp.float32), kept.astype(jnp.float32)),
            )
            odd = odd + sums[pair, count - 2].astype(jnp.float32)
            for t in range(3):
                at = t * D + pair * PAIR
                a = pl.ds(pl.multiple_of(at + core * HALF, PAIR), PAIR)
                b = pl.ds(pl.multiple_of(at + (1 - core) * HALF, PAIR), PAIR)
                pg_ref[:, a] = even[:, t * PAIR : (t + 1) * PAIR] * grad_scale
                pg_ref[:, b] = odd[:, t * PAIR : (t + 1) * PAIR] * grad_scale

        sum_pair(0)
        sum_pair(1)
        own_copy().wait()
        for j in range(chunks):
            x_copy(j).wait_send()
        ng_ref[...] = acc[pl.ds(W + mine_at, half), :] + yr[...].astype(jnp.float32)
        sum_pair(2)
        for j in range(chunks):

            @pl.when(me >= 2)
            def _():
                fwd_copy(j).wait_send()

            @pl.when(me < count - 2)
            def _():
                fwd_copy(j).wait_recv()
                ng_ref[j * piece : (j + 1) * piece, :] += later[j].astype(jnp.float32)


def fused(count, grad_scale, nx, weights, cosine, sine, seg_q, seg_k, out_grads):
    half = nx.shape[0]
    own = 2 * half
    total = own + W
    pairs = HALF // PAIR
    share = D // count
    chunks = 4
    whole = pl.BlockSpec(memory_space=pltpu.VMEM)

    bf16, f32 = jnp.bfloat16, jnp.float32
    return pl.pallas_call(
        functools.partial(fused_kernel, count=count, grad_scale=grad_scale),
        out_shape=[
            jax.ShapeDtypeStruct((half, D), bf16),
            jax.ShapeDtypeStruct((half, D), f32),
            jax.ShapeDtypeStruct((share, 3 * D), f32),
        ],
        grid=(pairs,),
        in_specs=[whole] * 7,
        out_specs=[whole, whole, whole],
        scratch_shapes=[
            pltpu.VMEM((total, D), bf16),
            pltpu.VMEM((pairs, D, 3 * PAIR), bf16),
            pltpu.VMEM((pairs, own, PAIR), bf16),
            pltpu.SemaphoreType.DMA((pairs, count - 1)),
            pltpu.SemaphoreType.DMA((pairs, count - 1)),
            pltpu.SemaphoreType.DMA((3,)),
            pltpu.SemaphoreType.DMA((3,)),
            pltpu.SemaphoreType.DMA((pairs,)),
            pltpu.SemaphoreType.DMA((pairs,)),
            pltpu.VMEM((own // BLOCK, BLOCK, SPAN), f32),
            pltpu.VMEM((own, PAIR), bf16),
            pltpu.VMEM((total, PAIR), bf16),
            pltpu.VMEM((total, PAIR), bf16),
            pltpu.VMEM((total, PAIR), f32),
            pltpu.VMEM((total, PAIR), f32),
            pltpu.VMEM((own, PAIR), bf16),
            pltpu.VMEM((total, 2 * PAIR), bf16),
            pltpu.VMEM((pairs, own, PAIR), bf16),
            pltpu.VMEM((pairs, half, PAIR), bf16),
            pltpu.VMEM((total, D), f32),
            pltpu.VMEM((pairs, D, 3 * PAIR), bf16),
            pltpu.VMEM((pairs, count - 1, share, 3 * PAIR), bf16),
            pltpu.VMEM((chunks, half // chunks, D), bf16),
            pltpu.VMEM((chunks, half // chunks, D), bf16),
            pltpu.VMEM((half, D), bf16),
            pltpu.VMEM((half, D), bf16),
            pltpu.VMEM((chunks, half // chunks, D), bf16),
            pltpu.VMEM((chunks, half // chunks, D), bf16),
            pltpu.SemaphoreType.DMA((pairs, count - 1)),
            pltpu.SemaphoreType.DMA((pairs, count - 1)),
            pltpu.SemaphoreType.DMA((pairs,)),
            pltpu.SemaphoreType.DMA((pairs,)),
            pltpu.SemaphoreType.DMA((chunks + 1,)),
            pltpu.SemaphoreType.DMA((chunks + 1,)),
            pltpu.SemaphoreType.DMA((chunks,)),
            pltpu.SemaphoreType.DMA((chunks,)),
        ],
        compiler_params=pltpu.CompilerParams(
            vmem_limit_bytes=56 * 1024 * 1024, collective_id=0, has_side_effects=True
        ),
        name="fused_attention",
    )(nx, weights, cosine, sine, seg_q, seg_k, out_grads)


def tables(meta_all, chip):
    half_size = HD // 2
    frequency = jnp.exp(-math.log(10000.0) * jnp.arange(half_size, dtype=jnp.float32) / half_size)
    angle = meta_all[0].astype(jnp.float32)[:, None] * frequency[None, :]
    c, s = jnp.cos(angle), jnp.sin(angle)
    cosine = jnp.concatenate([c, c, c, c], axis=1)
    sine = jnp.concatenate([-s, s, -s, s], axis=1)
    seg_all = meta_all[1]
    outside = (jnp.arange(seg_all.shape[0]) < W) & (chip == 0)
    seg_k = jnp.where(outside, -1, seg_all)[None, :]
    seg_q = seg_all[W:][:, None]
    return cosine, sine, seg_q, seg_k


def swapped(value):
    count = lax.axis_size("seq")
    return lax.ppermute(value, "seq", [(s, s ^ 1) for s in range(count)])


def chip_shifted(value, steps):
    count = lax.axis_size("seq")
    pairs = [(s, s + 2 * steps) for s in range(count) if 0 <= s + 2 * steps < count]
    return lax.ppermute(value, "seq", pairs)


def ordered(core, mine, other, axis=0):
    first = jnp.where(core == 0, mine, other)
    second = jnp.where(core == 0, other, mine)
    return jnp.concatenate([first, second], axis=axis)


def local(inputs, projection, positions, segments, context_grad):
    row_count = inputs.shape[0]
    device_count = lax.axis_size("seq")
    chips = device_count // 2
    device_index = lax.axis_index("seq")
    core = device_index % 2
    chip = device_index // 2
    assert 2 * row_count == W
    grad_scale = (row_count * device_count) ** (-0.5)

    meta = jnp.stack([positions, segments], axis=0)
    x_float = inputs.astype(jnp.float32)
    inv_rms = lax.rsqrt(jnp.mean(x_float * x_float, axis=1, keepdims=True) + EPSILON)
    scaled = x_float * inv_rms

    if (D // device_count) % 16 == 0:
        crossed = [(s, (s + 2) ^ 1) for s in range(device_count - 2)]
        meta_all = jnp.concatenate(
            [
                ordered(core, chip_shifted(meta, 1), lax.ppermute(meta, "seq", crossed), 1),
                ordered(core, meta, swapped(meta), 1),
            ],
            axis=1,
        )
        cosine, sine, seg_q, seg_k = tables(meta_all, chip)
        pieces = projection.reshape(D // device_count, 3, 2, 3, PAIR)
        pieces = jnp.transpose(pieces, (2, 3, 0, 1, 4)).reshape(2, 3, D // device_count, 3 * PAIR)
        context, normed_grad, projection_grad = fused(
            device_count, grad_scale, scaled.astype(jnp.bfloat16), pieces, cosine, sine, seg_q,
            seg_k, context_grad,
        )
        input_grad = (
            inv_rms * (normed_grad - scaled * jnp.mean(normed_grad * scaled, axis=1, keepdims=True))
        ).astype(jnp.bfloat16)
        return (context, input_grad, projection_grad)

    weights = lax.all_gather(projection, "seq", axis=0, tiled=True)
    x_before = chip_shifted(inputs, 1)
    meta_before = chip_shifted(meta, 1)
    x_other = swapped(inputs)
    meta_other = swapped(meta)
    x_before_other = swapped(x_before)
    meta_before_other = swapped(meta_before)
    grad_mine = lax.dynamic_slice_in_dim(context_grad, core * HALF, HALF, 1)
    grad_sent = lax.dynamic_slice_in_dim(context_grad, (1 - core) * HALF, HALF, 1)
    grad_other = swapped(grad_sent)
    out_grads = ordered(core, grad_mine, grad_other)

    x_all = jnp.concatenate(
        [ordered(core, x_before, x_before_other), ordered(core, inputs, x_other)], axis=0
    ).astype(jnp.float32)
    nx = (
        x_all * lax.rsqrt(jnp.mean(x_all * x_all, axis=1, keepdims=True) + EPSILON)
    ).astype(jnp.bfloat16)
    meta_all = jnp.concatenate(
        [ordered(core, meta_before, meta_before_other, 1), ordered(core, meta, meta_other, 1)],
        axis=1,
    )
    cosine, sine, seg_q, seg_k = tables(meta_all, chip)
    context_heads, dq, dk, dv = attention(
        core.astype(jnp.int32)[None], nx, weights, cosine, sine, seg_q, seg_k, out_grads
    )

    mine_at = core * row_count
    other_at = (1 - core) * row_count
    context_mine = lax.dynamic_slice_in_dim(context_heads, mine_at, row_count, 0)
    context_other = swapped(lax.dynamic_slice_in_dim(context_heads, other_at, row_count, 0))
    context = ordered(core, context_mine, context_other, 1)

    w_q, w_k, w_v = [
        lax.dynamic_slice_in_dim(weights, t * D + core * HALF, HALF, 1) for t in range(3)
    ]
    dkv = jnp.concatenate([dk, dv], axis=1)
    w_kv = jnp.concatenate([w_k, w_v], axis=1)
    ng_kv = contract(dkv, w_kv, 1, 1)
    ng_q = contract(dq, w_q, 1, 1)
    ng_before = ng_kv[:W]
    ng_own = ng_kv[W:] + ng_q
    send_before = lax.dynamic_slice_in_dim(ng_before, other_at, row_count, 0).astype(jnp.bfloat16)
    keep_before = lax.dynamic_slice_in_dim(ng_before, mine_at, row_count, 0)
    before = keep_before + swapped(send_before).astype(jnp.float32)
    later = chip_shifted(before.astype(jnp.bfloat16), -1)
    send_own = lax.dynamic_slice_in_dim(ng_own, other_at, row_count, 0).astype(jnp.bfloat16)
    keep_own = lax.dynamic_slice_in_dim(ng_own, mine_at, row_count, 0)
    normed_grad = (
        keep_own + swapped(send_own).astype(jnp.float32) + later.astype(jnp.float32)
    )
    input_grad = (
        inv_rms * (normed_grad - scaled * jnp.mean(normed_grad * scaled, axis=1, keepdims=True))
    ).astype(jnp.bfloat16)

    pg_kv = contract(nx, dkv, 0, 0)
    pg_q = contract(nx[W:], dq, 0, 0)
    pg = jnp.concatenate([pg_q, pg_kv], axis=1).astype(jnp.bfloat16)
    groups = [[2 * i + k for i in range(chips)] for k in range(2)]
    summed = lax.psum_scatter(
        pg, "seq", scatter_dimension=0, axis_index_groups=groups, tiled=True
    ).astype(jnp.float32)
    rows = summed.shape[0] // 2
    keep = lax.dynamic_slice_in_dim(summed, core * rows, rows, 0)
    other = swapped(lax.dynamic_slice_in_dim(summed, (1 - core) * rows, rows, 0).astype(jnp.bfloat16))
    other = other.astype(jnp.float32)
    parts = []
    for t in range(3):
        cols = slice(t * HALF, (t + 1) * HALF)
        parts.append(ordered(core, keep[:, cols], other[:, cols], 1))
    projection_grad = jnp.concatenate(parts, axis=1) * grad_scale
    return (context, input_grad, projection_grad)


def solution(mesh):
    in_specs = (
        P(("groups", "seq"), None),
        P("seq", None),
        P(("groups", "seq")),
        P(("groups", "seq")),
        P(("groups", "seq"), None),
    )
    out_specs = (P(("groups", "seq"), None), P(("groups", "seq"), None), P(("groups", "seq"), None))
    return jax.shard_map(local, mesh=mesh, in_specs=in_specs, out_specs=out_specs, check_vma=False)
```
